256 devices in a mesh: row: 16 (over y_lo, z), col: 16 (over x, y_hi, core).
Axes of the slice: x: 4, y: 4 (y_hi: 2, y_lo: 2; y = y_hi * 2 + y_lo), z: 8, core: 2. Of those that a mesh axis runs over, the one named last changes fastest.
Arguments:
- residual: float32 [512, 512, 256], P('row', 'col'), may hold values from -6 to 6
- adjoint: float32 [512, 512, 256], P('row', 'col'), may hold values from -6 to 6
- coefficient: bfloat16 [512, 512, 256], P('row', 'col'), may hold values from 0.25 to 4
- basis_x: float32 [512, 512], replicated, may hold values from -0.25 to 0.25
- basis_y: float32 [512, 512], replicated, may hold values from -0.25 to 0.25
- basis_z: float32 [256, 256], replicated, may hold values from -0.375 to 0.375
- eigen_x: float32 [512], replicated, may hold values from 0.02 to 2
- eigen_y: float32 [512], replicated, may hold values from 0.02 to 2
- eigen_z: float32 [256], replicated, may hold values from 0.02 to 2
Outputs:
- adjoint_next: float32 [512, 512, 256], P('row', 'col')
- residual_next: float32 [512, 512, 256], P('row', 'col')
The draws below stay inside these ranges and needn't reach their ends.
All inputs are finite; a program needn't handle non-finite values.
Results may differ from the reference program's by a relative error of at most 0.0003.
Values sent between devices are 32-bit elements; how exact they have to be, the bound alone decides.
A program may use at most 64 MiB of HBM per device.

```python
import math
import jax
import jax.numpy as jnp
from jax import lax

NX = 512
NY = 512
NZ = 256


def shard_levels(own_key, extent, split, low, high):
    def one(dim, blocks):
        steps = jax.random.uniform(jax.random.fold_in(jax.random.fold_in(own_key, 6), dim), (blocks,), jnp.float32, low / len(split), high / len(split))
        return jnp.repeat(jnp.exp(steps), extent[dim] // blocks).reshape((-1,) + (1,) * (len(extent) - dim - 1))

    level = one(*split[0])
    for cut in split[1:]:
        level = level * one(*cut)
    return level


def bell_draw(own_key, dims, width, reach, pieces=(), kind=jnp.bfloat16):
    level = shard_levels(own_key, dims, pieces, -0.22, 0.18) if pieces else 1.0
    array = jax.random.normal(own_key, dims, jnp.float32) * width * level
    return jnp.minimum(jnp.maximum(array, -reach), reach).astype(kind)


def setup_inputs(seed: int = 0) -> dict:
    key_of = jax.random.split(jax.random.key(seed), 10)
    return {
        "residual": bell_draw(key_of[0], (NX, NY, NZ), 1.0, 6.0, ((0, 16), (1, 16)), jnp.float32),
        "adjoint": bell_draw(key_of[1], (NX, NY, NZ), 1.0, 6.0, ((0, 16), (1, 16)), jnp.float32),
        "coefficient": jnp.clip(jnp.exp(math.log(4.0) - 2.7725887 * jax.random.uniform(key_of[2], (NX, NY, NZ), jnp.float32) ** shard_levels(key_of[2], (NX, NY, NZ), ((0, 16), (1, 16)), -0.2, 0.2)), 0.25, 4.0).astype(jnp.bfloat16),
        "basis_x": bell_draw(key_of[3], (NX, NX), NX ** -0.5, 0.25, (), jnp.float32),
        "basis_y": bell_draw(key_of[4], (NY, NY), NY ** -0.5, 0.25, (), jnp.float32),
        "basis_z": bell_draw(key_of[5], (NZ, NZ), NZ ** -0.5, 0.375, (), jnp.float32),
        "eigen_x": jnp.clip(jnp.exp(jax.random.uniform(key_of[6], (NX,), jnp.float32, math.log(0.02), math.log(2.0))), 0.02, 2.0),
        "eigen_y": jnp.clip(jnp.exp(jax.random.uniform(key_of[7], (NY,), jnp.float32, math.log(0.02), math.log(2.0))), 0.02, 2.0),
        "eigen_z": jnp.clip(jnp.exp(jax.random.uniform(key_of[8], (NZ,), jnp.float32, math.log(0.02), math.log(2.0))), 0.02, 2.0),
    }


MASS_TAPS = (1.0 / 5040, 120.0 / 5040, 1191.0 / 5040, 2416.0 / 5040, 1191.0 / 5040, 120.0 / 5040, 1.0 / 5040)
STIFF_TAPS = (-1.0 / 120, -0.2, -0.125, 2.0 / 3.0, -0.125, -0.2, -1.0 / 120)


def taps_along(padded, coeffs, axis_dim, length):
    running = coeffs[0] * lax.slice_in_dim(padded, 0, length, axis=axis_dim)
    for offset in range(1, 7):
        running = running + coeffs[offset] * lax.slice_in_dim(padded, offset, offset + length, axis=axis_dim)
    return running


def stiffness(padded, length_x, length_y, length_z):
    mass_x = taps_along(padded, MASS_TAPS, 0, length_x)
    stiff_x = taps_along(padded, STIFF_TAPS, 0, length_x)
    mass_xy = taps_along(mass_x, MASS_TAPS, 1, length_y)
    stiff_y = taps_along(mass_x, STIFF_TAPS, 1, length_y)
    stiff_xm = taps_along(stiff_x, MASS_TAPS, 1, length_y)
    return taps_along(stiff_y + stiff_xm, MASS_TAPS, 2, length_z) + taps_along(mass_xy, STIFF_TAPS, 2, length_z)


def reference(residual, adjoint, coefficient, basis_x, basis_y, basis_z, eigen_x, eigen_y, eigen_z):
    highest = lax.Precision.HIGHEST
    spectrum = jnp.einsum('xyz,zc->xyc', residual, basis_z, precision=highest)
    spectrum = jnp.einsum('xyc,yb->xbc', spectrum, basis_y, precision=highest)
    spectrum = jnp.einsum('xbc,xa->abc', spectrum, basis_x, precision=highest)
    denominator = eigen_x[:, None, None] + eigen_y[None, :, None] + eigen_z[None, None, :]
    scaled = spectrum / denominator
    correction = jnp.einsum('abc,xa->xbc', scaled, basis_x, precision=highest)
    correction = jnp.einsum('xbc,yb->xyc', correction, basis_y, precision=highest)
    correction = jnp.einsum('xyc,zc->xyz', correction, basis_z, precision=highest)
    weighted = coefficient.astype(jnp.float32) * correction
    padded = jnp.pad(weighted, 3)
    image = stiffness(padded, NX, NY, NZ)
    return adjoint + correction, residual - image
```

```python
import jax
import jax.numpy as jnp
from jax import lax
from jax.experimental import pallas as pl
from jax.experimental.pallas import tpu as pltpu
from jax.sharding import PartitionSpec as P

MESH = pl.DeviceIdType.MESH
F32, BF16 = jnp.float32, jnp.bfloat16
N = 16
Q = 4
ROWS = 48
MASS = (2416.0, 1191.0, 120.0, 1.0)
STIFF = (80.0, -15.0, -24.0, -1.0)


def split(x):
    hi = x.astype(BF16)
    return hi, (x - hi.astype(F32)).astype(BF16)


def dot3(a, b, dims=((1,), (0,))):
    (ah, al), (bh, bl) = a, b

    def one(u, v):
        return lax.dot_general(u, v, (dims, ((), ())), preferred_element_type=F32)

    return one(ah, bh) + (one(ah, bl) + one(al, bh))


def transpose4(a):
    lane = lax.broadcasted_iota(jnp.int32, a[0].shape, 1)
    low, even = lane < 64, (lane & 32) == 0
    half = [pltpu.roll(v, 64, 1) for v in a]
    c = [
        jnp.where(low, a[0], half[2]),
        jnp.where(low, a[1], half[3]),
        jnp.where(low, half[0], a[2]),
        jnp.where(low, half[1], a[3]),
    ]
    return [
        jnp.where(even, c[0], pltpu.roll(c[1], 32, 1)),
        jnp.where(even, pltpu.roll(c[0], 96, 1), c[1]),
        jnp.where(even, c[2], pltpu.roll(c[3], 32, 1)),
        jnp.where(even, pltpu.roll(c[2], 96, 1), c[3]),
    ]


def taps(coeffs, scale, planes):
    total = (coeffs[0] * scale) * planes[0]
    for d in range(1, 4):
        total = total + (coeffs[d] * scale) * planes[d]
    return total


def band(coeffs, scale, n):
    i = lax.broadcasted_iota(jnp.int32, (n, n), 0)
    j = lax.broadcasted_iota(jnp.int32, (n, n), 1)
    dist = jnp.abs(i - j)
    total = jnp.zeros((n, n), F32)
    for d in range(4):
        total = jnp.where(dist == d, coeffs[d] * scale, total)
    return total


def kernel(
    res_ref, bz_ref, ex_ref, ey_ref, ez_ref, coef_any, bx_any, by_any,
    corr_ref, image_ref,
    coef, bx, by,
    lh, ll, lmh, lml, byh, byl, bxh, bxl, bxth, bxtl, zh, zl, ext, rowv,
    send_c, recv_c, send_r, recv_r, send_rb, recv_rb, send_cb, recv_cb,
    fbuf, ubuf, acc, wext, ypack, yrecv, corner, mixed,
    in_sem, send_sem, recv_sem, hsend_sem, hrecv_sem,
):
    r, n = lax.axis_index("row"), lax.axis_index("col")

    loads = [
        pltpu.make_async_copy(src, dst, in_sem.at[s])
        for s, (src, dst) in enumerate(((by_any, by), (bx_any, bx), (coef_any, coef)))
    ]
    for load in loads:
        load.start()

    barrier = pltpu.get_barrier_semaphore()

    def greet(d, _):
        pl.semaphore_signal(barrier, inc=1, device_id=(r, lax.rem(n + d, N)), device_id_type=MESH)
        pl.semaphore_signal(barrier, inc=1, device_id=(lax.rem(r + d, N), n), device_id_type=MESH)
        return 0

    lax.fori_loop(1, N, greet, 0)
    for dr in (1, N - 1):
        for dn in (1, N - 1):
            pl.semaphore_signal(
                barrier, inc=1, device_id=(lax.rem(r + dr, N), lax.rem(n + dn, N)), device_id_type=MESH
            )

    bzt = bz_ref[...].T
    top = lax.broadcasted_iota(jnp.int32, (8, 256), 0) < 4
    for p in range(32):
        v = bzt[8 * p : 8 * p + 8, :]
        w = pltpu.roll(v, 4, 0)
        for s, rows in enumerate((jnp.where(top, v, w), jnp.where(top, w, v))):
            at = pl.ds(16 * p + 8 * s, 8)
            fbuf[0, at, :] = rows[:, :128]
            fbuf[1, at, :] = rows[:, 128:]
    lmat = jnp.concatenate([fbuf[0], fbuf[1]], axis=1)
    lmat_h, lmat_l = split(lmat)
    lh[...] = lmat_h
    ll[...] = lmat_l

    def exchange(stage, k, src, dst, over_row):
        mine = r if over_row else n

        def one(d, _):
            peer = lax.rem(mine + d, N)
            pltpu.make_async_remote_copy(
                src_ref=src.at[k, peer],
                dst_ref=dst.at[k, mine],
                send_sem=send_sem.at[stage, k],
                recv_sem=recv_sem.at[stage, k],
                device_id=(peer, n) if over_row else (r, peer),
                device_id_type=MESH,
            ).start()
            return 0

        lax.fori_loop(1, N, one, 0)
        pltpu.make_async_copy(src.at[k, mine], dst.at[k, mine], recv_sem.at[stage, k]).start()

    def arrived(stage, k, dst):
        pltpu.make_async_copy(dst.at[k], dst.at[k], recv_sem.at[stage, k]).wait()

    data = [split(res_ref[16 * h : 16 * h + 16].reshape(512, 256)) for h in range(2)]
    top16 = lax.broadcasted_iota(jnp.int32, (N, 8, 512), 1) < 4
    for k in range(Q):
        rows = (lh[128 * k : 128 * k + 128, :], ll[128 * k : 128 * k + 128, :])
        a, b = (dot3(rows, data[h], ((1,), (1,))).reshape(N, 8, 512) for h in range(2))
        send_c[k] = jnp.where(top16, a, b)
        if k == 0:
            pl.semaphore_wait(barrier, 2 * (N - 1) + 4)
        exchange(0, k, send_c, recv_c, False)

    loads[0].wait()
    byh[...], byl[...] = split(by[...])
    loads[1].wait()
    bxh[...], bxl[...] = split(bx[...])
    bxth[...], bxtl[...] = split(bx[...].T)
    half0 = (lax.broadcasted_iota(jnp.int32, (512, 256), 0) & 4) == 0
    lm_h, lm_l = split(jnp.concatenate([jnp.where(half0, lmat, 0.0), jnp.where(half0, 0.0, lmat)], axis=1))
    lmh[...], lml[...] = lm_h, lm_l
    zh[:256, :], zl[:256, :] = split(band(MASS, 1.0 / 5040, 256))
    zh[256:, :], zl[256:, :] = split(band(STIFF, 1.0 / 120, 256))
    ext[...] = jnp.broadcast_to(ex_ref[...], (128, 512)).T
    lane = lax.broadcasted_iota(jnp.int32, (8, 128), 1)
    ey = pltpu.roll(jnp.broadcast_to(ey_ref[...], (8, 512)), lax.rem((N - r) * 32, 512), 1)[:, :128]
    ey = jnp.where(lane < 32, ey, 0.0)
    ey = ey + pltpu.roll(ey, 32, 1)
    ey = ey + pltpu.roll(ey, 64, 1)
    zlane = lax.broadcasted_iota(jnp.int32, (8, 256), 1)
    ez = jnp.broadcast_to(ez_ref[...], (8, 256))
    for k in range(Q):
        row = ey
        for c in range(4):
            one = jnp.sum(jnp.where(zlane == k * 64 + n * 4 + c, ez, 0.0), axis=1, keepdims=True)
            row = row + jnp.where((lane >= 32 * c) & (lane < 32 * c + 32), one, 0.0)
        rowv[k] = row

    def stage_y(k):
        arrived(0, k, recv_c)
        for g in range(4):
            for x in range(4):
                for t, v in enumerate(
                    transpose4([recv_c[k, 4 * g + m, :, 128 * x : 128 * x + 128] for m in range(4)])
                ):
                    fbuf[g, pl.ds(4 * x + t, 8, stride=16), :] = v
        f = jnp.concatenate([fbuf[g, :128, :] for g in range(4)], axis=1)
        s = dot3(split(f), (byh[...], byl[...]))
        for g in range(4):
            for x in range(2):
                blocks = [s[64 * x + 16 * c : 64 * x + 16 * c + 16, 128 * g : 128 * g + 128] for c in range(4)]
                for m, v in enumerate(transpose4(blocks)):
                    send_r[k, 4 * g + m, 16 * x : 16 * x + 16, :] = v
        exchange(1, k, send_r, recv_r, True)

    def stage_x(k):
        arrived(1, k, recv_r)
        spectrum = dot3((bxth[...], bxtl[...]), split(recv_r[k].reshape(512, 128)))
        scaled = spectrum / (ext[...] + rowv[k][:1, :])
        send_rb[k] = dot3((bxh[...], bxl[...]), split(scaled)).reshape(N, 32, 128)
        exchange(2, k, send_rb, recv_rb, True)

    def stage_yb(k):
        arrived(2, k, recv_rb)
        for g in range(4):
            for x in range(2):
                blocks = [recv_rb[k, 4 * g + m, 16 * x : 16 * x + 16, :] for m in range(4)]
                for c, v in enumerate(transpose4(blocks)):
                    ubuf[64 * x + 16 * c : 64 * x + 16 * c + 16, 128 * g : 128 * g + 128] = v
        p = dot3(split(ubuf[...]), (byh[...], byl[...]), ((1,), (1,)))
        for g in range(4):
            fbuf[g, :128, :] = p[:, 128 * g : 128 * g + 128]
        for g in range(4):
            for x in range(4):
                blocks = [fbuf[g, pl.ds(4 * x + t, 8, stride=16), :] for t in range(4)]
                for m, v in enumerate(transpose4(blocks)):
                    send_cb[k, 4 * g + m, :, 128 * x : 128 * x + 128] = v
        exchange(3, k, send_cb, recv_cb, False)

    def stage_zb(k):
        arrived(3, k, recv_cb)
        t = split(recv_cb[k].reshape(128, 512).T)
        rows = pl.ds(pl.multiple_of(128 * k, 128), 128)
        part = dot3(t, (lmh[rows, :], lml[rows, :]))
        for h in range(2):
            acc[512 * h : 512 * h + 512, :] = acc[512 * h : 512 * h + 512, :] + part[:, 256 * h : 256 * h + 256]

    acc[...] = jnp.zeros((1024, 256), F32)

    def step(s, _):
        @pl.when(s < Q)
        def _():
            stage_y(s)

        @pl.when((s >= 1) & (s < Q + 1))
        def _():
            stage_x(s - 1)

        @pl.when((s >= 3) & (s < Q + 3))
        def _():
            stage_yb(s - 3)

        @pl.when(s >= 5)
        def _():
            stage_zb(s - 5)

        return 0

    lax.fori_loop(0, Q + 5, step, 0)

    loads[2].wait()
    for x in range(32):
        c = acc[32 * x : 32 * x + 32, :]
        corr_ref[x] = c
        w = coef[x].astype(F32) * c
        at = pl.ds(ROWS * (x + 3) + 8, 32)
        wext[0, at, :] = w[:, :128]
        wext[1, at, :] = w[:, 128:]
    for side, first in ((0, 8), (1, 37)):
        for d in range(3):
            for h in range(2):
                ypack[side, d, h] = wext[h, pl.ds(3 * ROWS + first + d, 32, stride=ROWS), :]

    has = {(0, 0): None}
    for dr in (-1, 0, 1):
        for dn in (-1, 0, 1):
            ok_r = (r > 0) if dr < 0 else (r < N - 1)
            ok_n = (n > 0) if dn < 0 else (n < N - 1)
            has[dr, dn] = ok_n if dr == 0 else ok_r if dn == 0 else ok_r & ok_n

    def copies(dr, dn):
        peer = (r + dr, n + dn)
        out = []
        if dn == 0:
            for d in range(3):
                src = pl.ds(ROWS * ((3 if dr < 0 else 32) + d) + 8, 32)
                dst = pl.ds(ROWS * ((35 if dr < 0 else 0) + d) + 8, 32)
                out.append((wext.at[:, src, :], wext.at[:, dst, :], (0 if dr < 0 else 3) + d))
        elif dr == 0:
            side = 0 if dn < 0 else 1
            out.append((ypack.at[side], yrecv.at[1 - side], 6 + side))
        else:
            side = 0 if dn < 0 else 1
            which = 2 * (1 if dr < 0 else 0) + (1 - side)
            rows = pl.ds(0 if dr < 0 else 24, 8)
            out.append((ypack.at[side, :, :, rows, :], corner.at[which], 8 + which))
        return [
            pltpu.make_async_remote_copy(
                src_ref=a, dst_ref=b, send_sem=hsend_sem.at[s], recv_sem=hrecv_sem.at[s],
                device_id=peer, device_id_type=MESH,
            )
            for a, b, s in out
        ]

    sides = [(dr, dn) for dr in (-1, 0, 1) for dn in (-1, 0, 1) if (dr, dn) != (0, 0)]
    for dr, dn in sides:

        @pl.when(has[dr, dn])
        def _():
            for c in copies(dr, dn):
                c.start()

    for dr in (-1, 1):

        @pl.when(jnp.logical_not(has[dr, 0]))
        def _():
            for d in range(3):
                at = pl.ds(ROWS * ((0 if dr < 0 else 35) + d) + 8, 32)
                for h in range(2):
                    wext[h, at, :] = jnp.zeros((32, 128), F32)

    for dn in (-1, 1):

        @pl.when(jnp.logical_not(has[0, dn]))
        def _():
            yrecv[0 if dn < 0 else 1] = jnp.zeros((3, 2, 32, 128), F32)

        for dr in (-1, 1):

            @pl.when(jnp.logical_not(has[dr, dn]))
            def _():
                corner[2 * (0 if dr < 0 else 1) + (0 if dn < 0 else 1)] = jnp.zeros((3, 2, 8, 128), F32)

    for dr, dn in sides:

        @pl.when(has[dr, dn])
        def _():
            for c in copies(-dr, -dn):
                c.wait_recv()

    for side, first in ((0, 5), (1, 40)):
        for d in range(3):
            for h in range(2):
                wext[h, pl.ds(3 * ROWS + first + d, 32, stride=ROWS), :] = yrecv[side, d, h]
                for low_or_high, plane, row in ((0, 0, 5), (1, 35, 0)):
                    for i in range(3):
                        wext[h, pl.ds(ROWS * (plane + i) + first + d, 1), :] = corner[
                            2 * low_or_high + side, d, h, row + i : row + i + 1, :
                        ]

    def stencil(x, _):
        base = pl.multiple_of(x * ROWS, 8)
        for h in range(2):
            p = [wext[h, pl.ds(base + ROWS * i, ROWS), :] for i in range(7)]
            sums = [p[3], p[2] + p[4], p[1] + p[5], p[0] + p[6]]

            def along_y(v):
                return [v[8:40]] + [
                    pltpu.roll(v, d, 0)[8:40] + pltpu.roll(v, ROWS - d, 0)[8:40] for d in range(1, 4)
                ]

            mass = along_y(taps(MASS, 1.0 / 5040, sums))
            stiff = along_y(taps(STIFF, 1.0 / 120, sums))
            at = pl.ds(pl.multiple_of(x * 32, 32), 32)
            mixed[at, 128 * h : 128 * h + 128] = taps(STIFF, 1.0 / 120, mass) + taps(MASS, 1.0 / 5040, stiff)
            mixed[at, 256 + 128 * h : 256 + 128 * h + 128] = taps(MASS, 1.0 / 5040, mass)
        return 0

    lax.fori_loop(0, 32, stencil, 0)
    for i in range(4):
        m = split(mixed[256 * i : 256 * i + 256, :])
        image_ref[8 * i : 8 * i + 8] = dot3(m, (zh[...], zl[...])).reshape(8, 32, 256)

    for dr, dn in sides:

        @pl.when(has[dr, dn])
        def _():
            for c in copies(dr, dn):
                c.wait_send()

    for stage, src in enumerate((send_c, send_r, send_rb, send_cb)):
        for k in range(Q):
            sent = src.at[k, pl.ds(0, N - 1)]
            pltpu.make_async_copy(sent, sent, send_sem.at[stage, k]).wait()


def shards(residual, adjoint, coefficient, basis_x, basis_y, basis_z, eigen_x, eigen_y, eigen_z):
    field = jax.ShapeDtypeStruct((32, 32, 256), F32)
    vmem = pl.BlockSpec(memory_space=pltpu.VMEM)
    hbm = pl.BlockSpec(memory_space=pl.ANY)
    wide, tall = pltpu.VMEM((Q, N, 8, 512), F32), pltpu.VMEM((Q, N, 32, 128), F32)
    square = pltpu.VMEM((512, 512), BF16)
    correction, image = pl.pallas_call(
        kernel,
        out_shape=(field, field),
        in_specs=[vmem] * 5 + [hbm] * 3,
        out_specs=(vmem, vmem),
        scratch_shapes=[
            pltpu.VMEM((32, 32, 256), BF16),
            pltpu.VMEM((512, 512), F32),
            pltpu.VMEM((512, 512), F32),
            pltpu.VMEM((512, 256), BF16),
            pltpu.VMEM((512, 256), BF16),
            square, square, square, square, square, square, square, square,
            pltpu.VMEM((512, 256), BF16),
            pltpu.VMEM((512, 256), BF16),
            pltpu.VMEM((512, 128), F32),
            pltpu.VMEM((Q, 8, 128), F32),
            wide, wide, tall, tall, tall, tall, wide, wide,
            pltpu.VMEM((4, 512, 128), F32),
            pltpu.VMEM((128, 512), F32),
            pltpu.VMEM((1024, 256), F32),
            pltpu.VMEM((2, 38 * ROWS, 128), F32),
            pltpu.VMEM((2, 3, 2, 32, 128), F32),
            pltpu.VMEM((2, 3, 2, 32, 128), F32),
            pltpu.VMEM((4, 3, 2, 8, 128), F32),
            pltpu.VMEM((1024, 512), F32),
            pltpu.SemaphoreType.DMA((3,)),
            pltpu.SemaphoreType.DMA((4, Q)),
            pltpu.SemaphoreType.DMA((4, Q)),
            pltpu.SemaphoreType.DMA((12,)),
            pltpu.SemaphoreType.DMA((12,)),
        ],
        compiler_params=pltpu.CompilerParams(
            collective_id=0, has_side_effects=True, vmem_limit_bytes=56 * 1024 * 1024
        ),
    )(
        residual, basis_z, eigen_x.reshape(1, 512), eigen_y.reshape(1, 512), eigen_z.reshape(1, 256),
        coefficient, basis_x, basis_y,
    )
    return adjoint + correction, residual - image


def solution(mesh):
    field = P("row", "col", None)
    return jax.shard_map(
        shards,
        mesh=mesh,
        in_specs=(field, field, field, P(), P(), P(), P(), P(), P()),
        out_specs=(field, field),
        check_vma=False,
    )
```

```python
import jax
import jax.numpy as jnp
from jax import lax
from jax.experimental import pallas as pl
from jax.experimental.pallas import tpu as pltpu
from jax.sharding import PartitionSpec as P

MESH = pl.DeviceIdType.MESH
F32, BF16 = jnp.float32, jnp.bfloat16
N = 16
Q = 4
ROWS = 48
MASS = (2416.0, 1191.0, 120.0, 1.0)
STIFF = (80.0, -15.0, -24.0, -1.0)


def split(x):
    hi = x.astype(BF16)
    return hi, (x - hi.astype(F32)).astype(BF16)


def dot3(a, b, dims=((1,), (0,))):
    (ah, al), (bh, bl) = a, b

    def one(u, v):
        return lax.dot_general(u, v, (dims, ((), ())), preferred_element_type=F32)

    return one(ah, bh) + (one(ah, bl) + one(al, bh))


def transpose4(a):
    lane = lax.broadcasted_iota(jnp.int32, a[0].shape, 1)
    low, even = lane < 64, (lane & 32) == 0
    half = [pltpu.roll(v, 64, 1) for v in a]
    c = [
        jnp.where(low, a[0], half[2]),
        jnp.where(low, a[1], half[3]),
        jnp.where(low, half[0], a[2]),
        jnp.where(low, half[1], a[3]),
    ]
    return [
        jnp.where(even, c[0], pltpu.roll(c[1], 32, 1)),
        jnp.where(even, pltpu.roll(c[0], 96, 1), c[1]),
        jnp.where(even, c[2], pltpu.roll(c[3], 32, 1)),
        jnp.where(even, pltpu.roll(c[2], 96, 1), c[3]),
    ]


def taps(coeffs, scale, planes):
    total = (coeffs[0] * scale) * planes[0]
    for d in range(1, 4):
        total = total + (coeffs[d] * scale) * planes[d]
    return total


def band(coeffs, scale, n):
    i = lax.broadcasted_iota(jnp.int32, (n, n), 0)
    j = lax.broadcasted_iota(jnp.int32, (n, n), 1)
    dist = jnp.abs(i - j)
    total = jnp.zeros((n, n), F32)
    for d in range(4):
        total = jnp.where(dist == d, coeffs[d] * scale, total)
    return total


def kernel(
    bz_hbm, res_hbm, ex_hbm, ey_hbm, ez_hbm, bx_hbm, by_hbm, coef_hbm,
    corr_ref, image_ref,
    bz, res, ex, ey, ez, bx, by, coef, dh, dl,
    lh, ll, lmh, lml, bh, bl, bth, btl, zh, zl, ext, rowv,
    send_c, recv_c, send_r, recv_r, send_rb, recv_rb, send_cb, recv_cb,
    fbuf, ubuf, acc, wext, ypack, yrecv, corner, mixed,
    in_sem, send_sem, recv_sem, hsend_sem, hrecv_sem,
):
    r, n = lax.axis_index("row"), lax.axis_index("col")

    loads = [
        pltpu.make_async_copy(src, dst, in_sem.at[s])
        for s, (src, dst) in enumerate(
            (
                (bz_hbm, bz), (res_hbm.at[:, :128], res.at[0]), (res_hbm.at[:, 128:], res.at[1]),
                (bx_hbm, bx), (by_hbm, by), (ex_hbm, ex), (ey_hbm, ey), (ez_hbm, ez), (coef_hbm, coef),
            )
        )
    ]
    for load in loads:
        load.start()

    barrier = pltpu.get_barrier_semaphore()

    def greet(d, _):
        pl.semaphore_signal(barrier, inc=1, device_id=(r, lax.rem(n + d, N)), device_id_type=MESH)
        pl.semaphore_signal(barrier, inc=1, device_id=(lax.rem(r + d, N), n), device_id_type=MESH)
        return 0

    lax.fori_loop(1, N, greet, 0)
    for dr in (1, N - 1):
        for dn in (1, N - 1):
            pl.semaphore_signal(
                barrier, inc=1, device_id=(lax.rem(r + dr, N), lax.rem(n + dn, N)), device_id_type=MESH
            )

    loads[0].wait()
    bzt = bz[...].T
    top = lax.broadcasted_iota(jnp.int32, (8, 256), 0) < 4
    for p in range(32):
        v = bzt[8 * p : 8 * p + 8, :]
        w = pltpu.roll(v, 4, 0)
        for s, rows in enumerate((jnp.where(top, v, w), jnp.where(top, w, v))):
            at = pl.ds(16 * p + 8 * s, 8)
            fbuf[0, at, :] = rows[:, :128]
            fbuf[1, at, :] = rows[:, 128:]
    lmat = jnp.concatenate([fbuf[0], fbuf[1]], axis=1)
    lmat_h, lmat_l = split(lmat)
    lh[...] = lmat_h
    ll[...] = lmat_l

    def exchange(stage, k, src, dst, over_row):
        mine = r if over_row else n

        def one(d, _):
            if over_row:
                peer = lax.rem(r // 8 + d // 8, 2) * 8 + lax.rem(r + d, 8)
            else:
                peer = lax.rem(n // 4 + d // 4, 4) * 4 + lax.rem(n // 2 + d // 2, 2) * 2 + lax.rem(n + d, 2)
            pltpu.make_async_remote_copy(
                src_ref=src.at[k, peer],
                dst_ref=dst.at[k, mine],
                send_sem=send_sem.at[stage, k],
                recv_sem=recv_sem.at[stage, k],
                device_id=(peer, n) if over_row else (r, peer),
                device_id_type=MESH,
            ).start()
            return 0

        lax.fori_loop(1, N, one, 0)
        pltpu.make_async_copy(src.at[k, mine], dst.at[k, mine], recv_sem.at[stage, k]).start()

    def arrived(stage, k, dst):
        pltpu.make_async_copy(dst.at[k], dst.at[k], recv_sem.at[stage, k]).wait()

    loads[1].wait()
    loads[2].wait()
    top16 = lax.broadcasted_iota(jnp.int32, (N, 8, 512), 1) < 4

    def stage_z(t, k):
        rows = (lh[128 * k : 128 * k + 128, :], ll[128 * k : 128 * k + 128, :])
        a, b = (
            dot3(rows, (dh[t, 512 * h : 512 * h + 512, :], dl[t, 512 * h : 512 * h + 512, :]), ((1,), (1,)))
            for h in range(2)
        )
        send_c[k] = jnp.where(top16, a.reshape(N, 8, 512), b.reshape(N, 8, 512))

    for y in range(32):
        plane = jnp.concatenate([res[h, pl.ds(y, 32, stride=32), :] for h in range(2)], axis=1)
        dh[0, 32 * y : 32 * y + 32, :], dl[0, 32 * y : 32 * y + 32, :] = split(plane)
    stage_z(0, 0)
    pl.semaphore_wait(barrier, 2 * (N - 1) + 4)
    exchange(0, 0, send_c, recv_c, True)
    dh[1], dl[1] = split(jnp.concatenate([res[0], res[1]], axis=1))
    stage_z(1, 2)
    exchange(0, 2, send_c, recv_c, False)
    stage_z(0, 1)
    exchange(0, 1, send_c, recv_c, True)
    stage_z(1, 3)
    exchange(0, 3, send_c, recv_c, False)

    loads[3].wait()
    loads[4].wait()
    for t, basis in enumerate((bx, by)):
        bh[t], bl[t] = split(basis[...])
        bth[t], btl[t] = split(basis[...].T)
    half0 = (lax.broadcasted_iota(jnp.int32, (512, 256), 0) & 4) == 0
    lmh[...], lml[...] = split(jnp.concatenate([jnp.where(half0, lmat, 0.0), jnp.where(half0, 0.0, lmat)], axis=1))
    zh[:256, :], zl[:256, :] = split(band(MASS, 1.0 / 5040, 256))
    zh[256:, :], zl[256:, :] = split(band(STIFF, 1.0 / 120, 256))
    for load in loads[5:8]:
        load.wait()
    lane = lax.broadcasted_iota(jnp.int32, (8, 128), 1)
    zlane = lax.broadcasted_iota(jnp.int32, (8, 256), 1)
    ezs = jnp.broadcast_to(ez[...], (8, 256))
    for t, (along, across, block, owner) in enumerate(((ey, ex, n, r), (ex, ey, r, n))):
        ext[t] = jnp.broadcast_to(along[...], (128, 512)).T
        own = pltpu.roll(jnp.broadcast_to(across[...], (8, 512)), lax.rem((N - block) * 32, 512), 1)[:, :128]
        own = jnp.where(lane < 32, own, 0.0)
        own = own + pltpu.roll(own, 32, 1)
        own = own + pltpu.roll(own, 64, 1)
        for k in (2 * t, 2 * t + 1):
            row = own
            for c in range(4):
                one = jnp.sum(jnp.where(zlane == k * 64 + owner * 4 + c, ezs, 0.0), axis=1, keepdims=True)
                row = row + jnp.where((lane >= 32 * c) & (lane < 32 * c + 32), one, 0.0)
            rowv[k] = row

    def first(t, k):
        arrived(0, k, recv_c)
        for g in range(4):
            for y in range(4):
                for u, v in enumerate(
                    transpose4([recv_c[k, 4 * g + m, :, 128 * y : 128 * y + 128] for m in range(4)])
                ):
                    fbuf[g, pl.ds(4 * y + u, 8, stride=16), :] = v
        f = jnp.concatenate([fbuf[g, :128, :] for g in range(4)], axis=1)
        s = dot3(split(f), (bh[t], bl[t]))
        for g in range(4):
            for y in range(2):
                blocks = [s[64 * y + 16 * c : 64 * y + 16 * c + 16, 128 * g : 128 * g + 128] for c in range(4)]
                for m, v in enumerate(transpose4(blocks)):
                    send_r[k, 4 * g + m, 16 * y : 16 * y + 16, :] = v
        exchange(1, k, send_r, recv_r, t == 1)

    def middle(t, k):
        arrived(1, k, recv_r)
        spectrum = dot3((bth[1 - t], btl[1 - t]), split(recv_r[k].reshape(512, 128)))
        scaled = spectrum / (ext[t] + rowv[k][:1, :])
        send_rb[k] = dot3((bh[1 - t], bl[1 - t]), split(scaled)).reshape(N, 32, 128)
        exchange(2, k, send_rb, recv_rb, t == 1)

    def first_back(t, k):
        arrived(2, k, recv_rb)
        for g in range(4):
            for y in range(2):
                blocks = [recv_rb[k, 4 * g + m, 16 * y : 16 * y + 16, :] for m in range(4)]
                for c, v in enumerate(transpose4(blocks)):
                    ubuf[64 * y + 16 * c : 64 * y + 16 * c + 16, 128 * g : 128 * g + 128] = v
        p = dot3(split(ubuf[...]), (bh[t], bl[t]), ((1,), (1,)))
        for g in range(4):
            fbuf[g, :128, :] = p[:, 128 * g : 128 * g + 128]
        for g in range(4):
            for y in range(4):
                blocks = [fbuf[g, pl.ds(4 * y + u, 8, stride=16), :] for u in range(4)]
                for m, v in enumerate(transpose4(blocks)):
                    send_cb[k, 4 * g + m, :, 128 * y : 128 * y + 128] = v
        exchange(3, k, send_cb, recv_cb, t == 0)

    def last(t, k):
        arrived(3, k, recv_cb)
        data = split(recv_cb[k].reshape(128, 512).T)
        rows = pl.ds(pl.multiple_of(128 * k, 128), 128)
        part = dot3(data, (lmh[rows, :], lml[rows, :]))
        for h in range(2):
            for w in range(2):
                at = pl.ds(512 * h, 512)
                acc[t, w, at, :] = acc[t, w, at, :] + part[:, 256 * h + 128 * w : 256 * h + 128 * w + 128]

    acc[...] = jnp.zeros((2, 2, 1024, 128), F32)

    def pairs(*steps):
        def one(j, _):
            for stage, t in steps:
                stage(t, 2 * t + j)
            return 0

        lax.fori_loop(0, 2, one, 0)

    pairs((first, 1), (first, 0))
    pairs((middle, 0), (middle, 1))
    pairs((first_back, 0))
    pairs((first_back, 1))
    pairs((last, 1), (last, 0))

    loads[8].wait()

    def weigh(x):
        for h in range(2):
            c = acc[0, h, pl.ds(x, 32, stride=32), :] + acc[1, h, 32 * x : 32 * x + 32, :]
            corr_ref[x, :, 128 * h : 128 * h + 128] = c
            wext[h, pl.ds(ROWS * (x + 3) + 8, 32), :] = coef[x, :, 128 * h : 128 * h + 128].astype(F32) * c

    has = {(0, 0): None}
    for dr in (-1, 0, 1):
        for dn in (-1, 0, 1):
            ok_r = (r > 0) if dr < 0 else (r < N - 1)
            ok_n = (n > 0) if dn < 0 else (n < N - 1)
            has[dr, dn] = ok_n if dr == 0 else ok_r if dn == 0 else ok_r & ok_n

    def copies(dr, dn):
        peer = (r + dr, n + dn)
        out = []
        if dn == 0:
            for d in range(3):
                src = pl.ds(ROWS * ((3 if dr < 0 else 32) + d) + 8, 32)
                dst = pl.ds(ROWS * ((35 if dr < 0 else 0) + d) + 8, 32)
                out.append((wext.at[:, src, :], wext.at[:, dst, :], (0 if dr < 0 else 3) + d))
        elif dr == 0:
            side = 0 if dn < 0 else 1
            out.append((ypack.at[side], yrecv.at[1 - side], 6 + side))
        else:
            side = 0 if dn < 0 else 1
            which = 2 * (1 if dr < 0 else 0) + (1 - side)
            rows = pl.ds(0 if dr < 0 else 24, 8)
            out.append((ypack.at[side, :, :, rows, :], corner.at[which], 8 + which))
        return [
            pltpu.make_async_remote_copy(
                src_ref=a, dst_ref=b, send_sem=hsend_sem.at[s], recv_sem=hrecv_sem.at[s],
                device_id=peer, device_id_type=MESH,
            )
            for a, b, s in out
        ]

    sides = [(dr, dn) for dr in (-1, 0, 1) for dn in (-1, 0, 1) if (dr, dn) != (0, 0)]
    def send(some):
        for dr, dn in some:

            @pl.when(has[dr, dn])
            def _():
                for c in copies(dr, dn):
                    c.start()

    for x in (0, 1, 2, 29, 30, 31):
        weigh(x)
    send([d for d in sides if d[1] == 0])
    for x in range(3, 29):
        weigh(x)
    for side, first in ((0, 8), (1, 37)):
        for d in range(3):
            for h in range(2):
                ypack[side, d, h] = wext[h, pl.ds(3 * ROWS + first + d, 32, stride=ROWS), :]
    send([d for d in sides if d[1] != 0])

    for dr in (-1, 1):

        @pl.when(jnp.logical_not(has[dr, 0]))
        def _():
            for d in range(3):
                at = pl.ds(ROWS * ((0 if dr < 0 else 35) + d) + 8, 32)
                for h in range(2):
                    wext[h, at, :] = jnp.zeros((32, 128), F32)

    for dn in (-1, 1):

        @pl.when(jnp.logical_not(has[0, dn]))
        def _():
            yrecv[0 if dn < 0 else 1] = jnp.zeros((3, 2, 32, 128), F32)

        for dr in (-1, 1):

            @pl.when(jnp.logical_not(has[dr, dn]))
            def _():
                corner[2 * (0 if dr < 0 else 1) + (0 if dn < 0 else 1)] = jnp.zeros((3, 2, 8, 128), F32)

    for dr, dn in sides:

        @pl.when(has[dr, dn])
        def _():
            for c in copies(-dr, -dn):
                c.wait_recv()

    for side, first in ((0, 5), (1, 40)):
        for d in range(3):
            for h in range(2):
                wext[h, pl.ds(3 * ROWS + first + d, 32, stride=ROWS), :] = yrecv[side, d, h]
                for low_or_high, plane, row in ((0, 0, 5), (1, 35, 0)):
                    for i in range(3):
                        wext[h, pl.ds(ROWS * (plane + i) + first + d, 1), :] = corner[
                            2 * low_or_high + side, d, h, row + i : row + i + 1, :
                        ]

    def stencil(x, _):
        base = pl.multiple_of(x * ROWS, 8)
        for h in range(2):
            p = [wext[h, pl.ds(base + ROWS * i, ROWS), :] for i in range(7)]
            sums = [p[3], p[2] + p[4], p[1] + p[5], p[0] + p[6]]

            def along_y(v):
                return [v[8:40]] + [
                    pltpu.roll(v, d, 0)[8:40] + pltpu.roll(v, ROWS - d, 0)[8:40] for d in range(1, 4)
                ]

            mass = along_y(taps(MASS, 1.0 / 5040, sums))
            stiff = along_y(taps(STIFF, 1.0 / 120, sums))
            at = pl.ds(pl.multiple_of(x * 32, 32), 32)
            mixed[at, 128 * h : 128 * h + 128] = taps(STIFF, 1.0 / 120, mass) + taps(MASS, 1.0 / 5040, stiff)
            mixed[at, 256 + 128 * h : 256 + 128 * h + 128] = taps(MASS, 1.0 / 5040, mass)
        return 0

    lax.fori_loop(0, 32, stencil, 0)
    for i in range(4):
        m = split(mixed[256 * i : 256 * i + 256, :])
        image_ref[8 * i : 8 * i + 8] = dot3(m, (zh[...], zl[...])).reshape(8, 32, 256)

    for dr, dn in sides:

        @pl.when(has[dr, dn])
        def _():
            for c in copies(dr, dn):
                c.wait_send()

    for stage, src in enumerate((send_c, send_r, send_rb, send_cb)):
        for k in range(Q):
            sent = src.at[k, pl.ds(0, N - 1)]
            pltpu.make_async_copy(sent, sent, send_sem.at[stage, k]).wait()


def shards(residual, adjoint, coefficient, basis_x, basis_y, basis_z, eigen_x, eigen_y, eigen_z):
    field = jax.ShapeDtypeStruct((32, 32, 256), F32)
    vmem = pl.BlockSpec(memory_space=pltpu.VMEM)
    hbm = pl.BlockSpec(memory_space=pltpu.HBM)
    wide, tall = pltpu.VMEM((Q, N, 8, 512), F32), pltpu.VMEM((Q, N, 32, 128), F32)
    square, pair = pltpu.VMEM((512, 512), BF16), pltpu.VMEM((2, 512, 512), BF16)
    correction, image = pl.pallas_call(
        kernel,
        out_shape=(field, field),
        in_specs=[hbm] * 8,
        out_specs=(vmem, vmem),
        scratch_shapes=[
            pltpu.VMEM((256, 256), F32),
            pltpu.VMEM((2, 1024, 128), F32),
            pltpu.VMEM((1, 512), F32),
            pltpu.VMEM((1, 512), F32),
            pltpu.VMEM((1, 256), F32),
            pltpu.VMEM((512, 512), F32),
            pltpu.VMEM((512, 512), F32),
            pltpu.VMEM((32, 32, 256), BF16),
            pltpu.VMEM((2, 1024, 256), BF16),
            pltpu.VMEM((2, 1024, 256), BF16),
            pltpu.VMEM((512, 256), BF16),
            pltpu.VMEM((512, 256), BF16),
            square, square, pair, pair, pair, pair,
            pltpu.VMEM((512, 256), BF16),
            pltpu.VMEM((512, 256), BF16),
            pltpu.VMEM((2, 512, 128), F32),
            pltpu.VMEM((Q, 8, 128), F32),
            wide, wide, tall, tall, tall, tall, wide, wide,
            pltpu.VMEM((4, 512, 128), F32),
            pltpu.VMEM((128, 512), F32),
            pltpu.VMEM((2, 2, 1024, 128), F32),
            pltpu.VMEM((2, 38 * ROWS, 128), F32),
            pltpu.VMEM((2, 3, 2, 32, 128), F32),
            pltpu.VMEM((2, 3, 2, 32, 128), F32),
            pltpu.VMEM((4, 3, 2, 8, 128), F32),
            pltpu.VMEM((1024, 512), F32),
            pltpu.SemaphoreType.DMA((9,)),
            pltpu.SemaphoreType.DMA((4, Q)),
            pltpu.SemaphoreType.DMA((4, Q)),
            pltpu.SemaphoreType.DMA((12,)),
            pltpu.SemaphoreType.DMA((12,)),
        ],
        compiler_params=pltpu.CompilerParams(
            collective_id=0, has_side_effects=True, vmem_limit_bytes=56 * 1024 * 1024
        ),
    )(
        basis_z, residual.reshape(1024, 256),
        eigen_x.reshape(1, 512), eigen_y.reshape(1, 512), eigen_z.reshape(1, 256),
        basis_x, basis_y, coefficient,
    )
    return adjoint + correction, residual - image


def solution(mesh):
    field = P("row", "col", None)
    return jax.shard_map(
        shards,
        mesh=mesh,
        in_specs=(field, field, field, P(), P(), P(), P(), P(), P()),
        out_specs=(field, field),
        check_vma=False,
    )
```

```python
import jax
import jax.numpy as jnp
from jax import lax
from jax.experimental import pallas as pl
from jax.experimental.pallas import tpu as pltpu
from jax.sharding import PartitionSpec as P

MESH = pl.DeviceIdType.MESH
F32, BF16 = jnp.float32, jnp.bfloat16
N = 16
Q = 4
ROWS = 48
MASS = (2416.0, 1191.0, 120.0, 1.0)
STIFF = (80.0, -15.0, -24.0, -1.0)


def split(x):
    hi = x.astype(BF16)
    return hi, (x - hi.astype(F32)).astype(BF16)


def dot3(a, b, dims=((1,), (0,))):
    (ah, al), (bh, bl) = a, b

    def one(u, v):
        return lax.dot_general(u, v, (dims, ((), ())), preferred_element_type=F32)

    return one(ah, bh) + (one(ah, bl) + one(al, bh))


def transpose4(a):
    lane = lax.broadcasted_iota(jnp.int32, a[0].shape, 1)
    low, even = lane < 64, (lane & 32) == 0
    half = [pltpu.roll(v, 64, 1) for v in a]
    c = [
        jnp.where(low, a[0], half[2]),
        jnp.where(low, a[1], half[3]),
        jnp.where(low, half[0], a[2]),
        jnp.where(low, half[1], a[3]),
    ]
    return [
        jnp.where(even, c[0], pltpu.roll(c[1], 32, 1)),
        jnp.where(even, pltpu.roll(c[0], 96, 1), c[1]),
        jnp.where(even, c[2], pltpu.roll(c[3], 32, 1)),
        jnp.where(even, pltpu.roll(c[2], 96, 1), c[3]),
    ]


def taps(coeffs, scale, planes):
    total = (coeffs[0] * scale) * planes[0]
    for d in range(1, 4):
        total = total + (coeffs[d] * scale) * planes[d]
    return total


def band(coeffs, scale, n):
    i = lax.broadcasted_iota(jnp.int32, (n, n), 0)
    j = lax.broadcasted_iota(jnp.int32, (n, n), 1)
    dist = jnp.abs(i - j)
    total = jnp.zeros((n, n), F32)
    for d in range(4):
        total = jnp.where(dist == d, coeffs[d] * scale, total)
    return total


def kernel(
    bz_hbm, res_hbm, ex_hbm, ey_hbm, ez_hbm, bx_hbm, by_hbm, coef_hbm, adj_hbm,
    adj_out, res_out,
    bz, res, ex, ey, ez, bx, by, coef, adj, dh, dl,
    lh, ll, lmh, lml, bh, bl, bth, btl, zh, zl, ext, rowv,
    send_c, recv_c, send_r, recv_r, send_rb, recv_rb, send_cb, recv_cb,
    fbuf, ubuf, acc, wext, ypack, hext, mixed,
    in_sem, out_sem, send_sem, recv_sem, hsend_sem, hrecv_sem,
):
    r, n = lax.axis_index("row"), lax.axis_index("col")

    loads = [
        pltpu.make_async_copy(src, dst, in_sem.at[s])
        for s, (src, dst) in enumerate(
            (
                (bz_hbm, bz), (res_hbm.at[:, :128], res.at[0]), (res_hbm.at[:, 128:], res.at[1]),
                (bx_hbm, bx), (by_hbm, by), (ex_hbm, ex), (ey_hbm, ey), (ez_hbm, ez), (coef_hbm, coef),
                (adj_hbm, adj),
            )
        )
    ]
    for load in loads:
        load.start()

    barrier = pltpu.get_barrier_semaphore()

    def greet(d, _):
        pl.semaphore_signal(barrier, inc=1, device_id=(r, lax.rem(n + d, N)), device_id_type=MESH)
        pl.semaphore_signal(barrier, inc=1, device_id=(lax.rem(r + d, N), n), device_id_type=MESH)
        return 0

    lax.fori_loop(1, N, greet, 0)
    for dr in (1, N - 1):
        for dn in (1, N - 1):
            pl.semaphore_signal(
                barrier, inc=1, device_id=(lax.rem(r + dr, N), lax.rem(n + dn, N)), device_id_type=MESH
            )

    loads[0].wait()
    top = lax.broadcasted_iota(jnp.int32, (8, 256), 0) < 4

    def prepare(t):
        bzt = bz[:, 128 * t : 128 * t + 128].T
        for p in range(16):
            v = bzt[8 * p : 8 * p + 8, :]
            w = pltpu.roll(v, 4, 0)
            for i, rows in enumerate((jnp.where(top, v, w), jnp.where(top, w, v))):
                at = pl.ds(256 * t + 16 * p + 8 * i, 8)
                fbuf[0, at, :] = rows[:, :128]
                fbuf[1, at, :] = rows[:, 128:]
        at = pl.ds(256 * t, 256)
        lh[at, :], ll[at, :] = split(jnp.concatenate([fbuf[0, at, :], fbuf[1, at, :]], axis=1))

    prepare(0)

    def exchange(stage, k, src, dst, over_row):
        mine = r if over_row else n

        def one(d, _):
            if over_row:
                peer = lax.rem(r // 8 + d // 8, 2) * 8 + lax.rem(r + d, 8)
            else:
                peer = lax.rem(n // 4 + d // 4, 4) * 4 + lax.rem(n // 2 + d // 2, 2) * 2 + lax.rem(n + d, 2)
            pltpu.make_async_remote_copy(
                src_ref=src.at[k, peer],
                dst_ref=dst.at[k, mine],
                send_sem=send_sem.at[stage, k],
                recv_sem=recv_sem.at[stage, k],
                device_id=(peer, n) if over_row else (r, peer),
                device_id_type=MESH,
            ).start()
            return 0

        lax.fori_loop(1, N, one, 0)
        pltpu.make_async_copy(src.at[k, mine], dst.at[k, mine], recv_sem.at[stage, k]).start()

    def arrived(stage, k, dst):
        pltpu.make_async_copy(dst.at[k], dst.at[k], recv_sem.at[stage, k]).wait()

    loads[1].wait()
    loads[2].wait()
    top16 = lax.broadcasted_iota(jnp.int32, (N, 8, 512), 1) < 4

    def stage_z(t, k):
        rows = (lh[128 * k : 128 * k + 128, :], ll[128 * k : 128 * k + 128, :])
        a, b = (
            dot3(rows, (dh[t, 512 * h : 512 * h + 512, :], dl[t, 512 * h : 512 * h + 512, :]), ((1,), (1,)))
            for h in range(2)
        )
        send_c[k] = jnp.where(top16, a.reshape(N, 8, 512), b.reshape(N, 8, 512))

    for y in range(32):
        plane = jnp.concatenate([res[h, pl.ds(y, 32, stride=32), :] for h in range(2)], axis=1)
        dh[0, 32 * y : 32 * y + 32, :], dl[0, 32 * y : 32 * y + 32, :] = split(plane)
    stage_z(0, 0)
    pl.semaphore_wait(barrier, 2 * (N - 1) + 4)
    exchange(0, 0, send_c, recv_c, True)
    prepare(1)
    dh[1], dl[1] = split(jnp.concatenate([res[0], res[1]], axis=1))
    stage_z(1, 2)
    exchange(0, 2, send_c, recv_c, False)
    stage_z(0, 1)
    exchange(0, 1, send_c, recv_c, True)
    stage_z(1, 3)
    exchange(0, 3, send_c, recv_c, False)

    loads[3].wait()
    loads[4].wait()
    for t, basis in enumerate((bx, by)):
        bh[t], bl[t] = split(basis[...])
        bth[t], btl[t] = split(basis[...].T)
    lmat = jnp.concatenate([fbuf[0], fbuf[1]], axis=1)
    half0 = (lax.broadcasted_iota(jnp.int32, (512, 256), 0) & 4) == 0
    lmh[...], lml[...] = split(jnp.concatenate([jnp.where(half0, lmat, 0.0), jnp.where(half0, 0.0, lmat)], axis=1))
    zh[:256, :], zl[:256, :] = split(band(MASS, 1.0 / 5040, 256))
    zh[256:, :], zl[256:, :] = split(band(STIFF, 1.0 / 120, 256))
    for load in loads[5:8]:
        load.wait()
    lane = lax.broadcasted_iota(jnp.int32, (8, 128), 1)
    zlane = lax.broadcasted_iota(jnp.int32, (8, 256), 1)
    ezs = jnp.broadcast_to(ez[...], (8, 256))
    for t, (along, across, block, owner) in enumerate(((ey, ex, n, r), (ex, ey, r, n))):
        ext[t] = jnp.broadcast_to(along[...], (128, 512)).T
        own = pltpu.roll(jnp.broadcast_to(across[...], (8, 512)), lax.rem((N - block) * 32, 512), 1)[:, :128]
        own = jnp.where(lane < 32, own, 0.0)
        own = own + pltpu.roll(own, 32, 1)
        own = own + pltpu.roll(own, 64, 1)
        for k in (2 * t, 2 * t + 1):
            row = own
            for c in range(4):
                one = jnp.sum(jnp.where(zlane == k * 64 + owner * 4 + c, ezs, 0.0), axis=1, keepdims=True)
                row = row + jnp.where((lane >= 32 * c) & (lane < 32 * c + 32), one, 0.0)
            rowv[k] = row

    def first(t, k):
        arrived(0, k, recv_c)
        for g in range(4):
            for y in range(4):
                for u, v in enumerate(
                    transpose4([recv_c[k, 4 * g + m, :, 128 * y : 128 * y + 128] for m in range(4)])
                ):
                    fbuf[g, pl.ds(4 * y + u, 8, stride=16), :] = v
        f = jnp.concatenate([fbuf[g, :128, :] for g in range(4)], axis=1)
        s = dot3(split(f), (bh[t], bl[t]))
        for g in range(4):
            for y in range(2):
                blocks = [s[64 * y + 16 * c : 64 * y + 16 * c + 16, 128 * g : 128 * g + 128] for c in range(4)]
                for m, v in enumerate(transpose4(blocks)):
                    send_r[k, 4 * g + m, 16 * y : 16 * y + 16, :] = v
        exchange(1, k, send_r, recv_r, t == 1)

    def middle(t, k):
        arrived(1, k, recv_r)
        spectrum = dot3((bth[1 - t], btl[1 - t]), split(recv_r[k].reshape(512, 128)))
        scaled = spectrum / (ext[t] + rowv[k][:1, :])
        send_rb[k] = dot3((bh[1 - t], bl[1 - t]), split(scaled)).reshape(N, 32, 128)
        exchange(2, k, send_rb, recv_rb, t == 1)

    def first_back(t, k):
        arrived(2, k, recv_rb)
        for g in range(4):
            for y in range(2):
                blocks = [recv_rb[k, 4 * g + m, 16 * y : 16 * y + 16, :] for m in range(4)]
                for c, v in enumerate(transpose4(blocks)):
                    ubuf[64 * y + 16 * c : 64 * y + 16 * c + 16, 128 * g : 128 * g + 128] = v
        p = dot3(split(ubuf[...]), (bh[t], bl[t]), ((1,), (1,)))
        for g in range(4):
            fbuf[g, :128, :] = p[:, 128 * g : 128 * g + 128]
        for g in range(4):
            for y in range(4):
                blocks = [fbuf[g, pl.ds(4 * y + u, 8, stride=16), :] for u in range(4)]
                for m, v in enumerate(transpose4(blocks)):
                    send_cb[k, 4 * g + m, :, 128 * y : 128 * y + 128] = v
        exchange(3, k, send_cb, recv_cb, t == 0)

    def last(t, k):
        arrived(3, k, recv_cb)
        data = split(recv_cb[k].reshape(128, 512).T)
        rows = pl.ds(pl.multiple_of(128 * k, 128), 128)
        part = dot3(data, (lmh[rows, :], lml[rows, :]))
        for h in range(2):
            for w in range(2):
                at = pl.ds(512 * h, 512)
                acc[t, w, at, :] = acc[t, w, at, :] + part[:, 256 * h + 128 * w : 256 * h + 128 * w + 128]

    acc[...] = jnp.zeros((2, 2, 1024, 128), F32)
    for x in range(38):
        for h in range(2):
            wext[h, ROWS * x : ROWS * x + 8, :] = jnp.zeros((8, 128), F32)
            wext[h, ROWS * x + 40 : ROWS * x + 48, :] = jnp.zeros((8, 128), F32)

    def pairs(*steps):
        def one(j, _):
            for stage, t in steps:
                stage(t, 2 * t + j)
            return 0

        lax.fori_loop(0, 2, one, 0)

    pairs((first, 1), (first, 0))
    pairs((middle, 0), (middle, 1))
    pairs((first_back, 0))
    pairs((first_back, 1))
    pairs((last, 1), (last, 0))

    loads[8].wait()

    def weigh(x):
        for h in range(2):
            c = acc[0, h, pl.ds(x, 32, stride=32), :] + acc[1, h, 32 * x : 32 * x + 32, :]
            wext[h, pl.ds(ROWS * (x + 3) + 8, 32), :] = coef[x, :, 128 * h : 128 * h + 128].astype(F32) * c

    has = {(0, 0): None}
    for dr in (-1, 0, 1):
        for dn in (-1, 0, 1):
            ok_r = (r > 0) if dr < 0 else (r < N - 1)
            ok_n = (n > 0) if dn < 0 else (n < N - 1)
            has[dr, dn] = ok_n if dr == 0 else ok_r if dn == 0 else ok_r & ok_n

    def copies(dr, dn):
        peer = (r + dr, n + dn)
        out = []
        if dn == 0:
            for d in range(3):
                src = pl.ds(ROWS * ((3 if dr < 0 else 32) + d) + 8, 32)
                dst = pl.ds(ROWS * ((35 if dr < 0 else 0) + d) + 8, 32)
                out.append((wext.at[:, src, :], wext.at[:, dst, :], (0 if dr < 0 else 3) + d))
        elif dr == 0:
            side = 0 if dn < 0 else 1
            out.append((ypack.at[side], hext.at[1 - side, :, :, pl.ds(8, 32), :], 6 + side))
        else:
            side = 0 if dn < 0 else 1
            rows, at = (0, 40) if dr < 0 else (24, 0)
            out.append(
                (
                    ypack.at[side, :, :, pl.ds(rows, 8), :],
                    hext.at[1 - side, :, :, pl.ds(at, 8), :],
                    8 + 2 * (dr > 0) + side,
                )
            )
        return [
            pltpu.make_async_remote_copy(
                src_ref=a, dst_ref=b, send_sem=hsend_sem.at[s], recv_sem=hrecv_sem.at[s],
                device_id=peer, device_id_type=MESH,
            )
            for a, b, s in out
        ]

    sides = [(dr, dn) for dr in (-1, 0, 1) for dn in (-1, 0, 1) if (dr, dn) != (0, 0)]
    def send(some):
        for dr, dn in some:

            @pl.when(has[dr, dn])
            def _():
                for c in copies(dr, dn):
                    c.start()

    for x in range(32):
        weigh(x)
    for side, first in ((0, 8), (1, 37)):
        for d in range(3):
            for h in range(2):
                ypack[side, d, h] = wext[h, pl.ds(3 * ROWS + first + d, 32, stride=ROWS), :]
    send([d for d in sides if d[0] == 0])
    send([d for d in sides if d[0] != 0])

    for dr in (-1, 1):

        @pl.when(jnp.logical_not(has[dr, 0]))
        def _():
            for d in range(3):
                at = pl.ds(ROWS * ((0 if dr < 0 else 35) + d) + 8, 32)
                for h in range(2):
                    wext[h, at, :] = jnp.zeros((32, 128), F32)

    for dn in (-1, 1):

        @pl.when(jnp.logical_not(has[0, dn]))
        def _():
            hext[0 if dn < 0 else 1, :, :, 8:40, :] = jnp.zeros((3, 2, 32, 128), F32)

        for dr in (-1, 1):

            @pl.when(jnp.logical_not(has[dr, dn]))
            def _():
                at = 0 if dr < 0 else 40
                hext[0 if dn < 0 else 1, :, :, at : at + 8, :] = jnp.zeros((3, 2, 8, 128), F32)

    loads[9].wait()
    for x in range(32):
        for h in range(2):
            c = acc[0, h, pl.ds(x, 32, stride=32), :] + acc[1, h, 32 * x : 32 * x + 32, :]
            at = slice(128 * h, 128 * h + 128)
            adj[32 * x : 32 * x + 32, at] = adj[32 * x : 32 * x + 32, at] + c
    stores = [pltpu.make_async_copy(adj, adj_out, out_sem.at[0])]
    stores[0].start()

    def receive(some):
        for dr, dn in some:

            @pl.when(has[dr, dn])
            def _():
                for c in copies(-dr, -dn):
                    c.wait_recv()

    receive([d for d in sides if d[1] == 0])

    def along_rows(v):
        return [v[8:40]] + [pltpu.roll(v, d, 0)[8:40] + pltpu.roll(v, ROWS - d, 0)[8:40] for d in range(1, 4)]

    def stencil(x, _):
        base = pl.multiple_of(x * ROWS, 8)
        for h in range(2):
            p = [wext[h, pl.ds(base + ROWS * i, ROWS), :] for i in range(7)]
            sums = [p[3], p[2] + p[4], p[1] + p[5], p[0] + p[6]]

            mass = along_rows(taps(MASS, 1.0 / 5040, sums))
            stiff = along_rows(taps(STIFF, 1.0 / 120, sums))
            at = pl.ds(pl.multiple_of(x * 32, 32), 32)
            mixed[at, 128 * h : 128 * h + 128] = taps(STIFF, 1.0 / 120, mass) + taps(MASS, 1.0 / 5040, stiff)
            mixed[at, 256 + 128 * h : 256 + 128 * h + 128] = taps(MASS, 1.0 / 5040, mass)
        return 0

    lax.fori_loop(0, 32, stencil, 0)
    for i in range(4):
        at = slice(256 * i, 256 * i + 256)
        image = dot3(split(mixed[at, :]), (zh[...], zl[...]))
        for h in range(2):
            res[h, at, :] = res[h, at, :] - image[:, 128 * h : 128 * h + 128]

    receive([d for d in sides if d[1] != 0])
    for side in range(2):
        for h in range(2):
            near = [along_rows(hext[side, d, h]) for d in range(3)]
            mass = [taps(MASS, 1.0 / 5040, v) for v in near]
            stiff = [taps(STIFF, 1.0 / 120, v) for v in near]
            for o in range(3):
                a = b = jnp.zeros((32, 128), F32)
                for d in range(o, 3) if side == 0 else range(o + 1):
                    dist = o + 3 - d if side == 0 else 3 + d - o
                    a = a + (STIFF[dist] / 120) * mass[d] + (MASS[dist] / 5040) * stiff[d]
                    b = b + (MASS[dist] / 5040) * mass[d]
                at = slice(96 * side + 32 * o, 96 * side + 32 * o + 32)
                mixed[at, 128 * h : 128 * h + 128] = a
                mixed[at, 256 + 128 * h : 256 + 128 * h + 128] = b
    image = dot3(split(mixed[:192, :]), (zh[...], zl[...]))
    for h in range(2):
        for side in range(2):
            for o in range(3):
                at = pl.ds(o if side == 0 else 29 + o, 32, stride=32)
                part = image[96 * side + 32 * o : 96 * side + 32 * o + 32, 128 * h : 128 * h + 128]
                res[h, at, :] = res[h, at, :] - part
        store = pltpu.make_async_copy(res.at[h], res_out.at[:, pl.ds(128 * h, 128)], out_sem.at[1 + h])
        store.start()
        stores.append(store)

    for dr, dn in sides:

        @pl.when(has[dr, dn])
        def _():
            for c in copies(dr, dn):
                c.wait_send()

    for stage, src in enumerate((send_c, send_r, send_rb, send_cb)):
        for k in range(Q):
            sent = src.at[k, pl.ds(0, N - 1)]
            pltpu.make_async_copy(sent, sent, send_sem.at[stage, k]).wait()

    for store in stores:
        store.wait()


def shards(residual, adjoint, coefficient, basis_x, basis_y, basis_z, eigen_x, eigen_y, eigen_z):
    field = jax.ShapeDtypeStruct((1024, 256), F32)
    hbm = pl.BlockSpec(memory_space=pltpu.HBM)
    wide, tall = pltpu.VMEM((Q, N, 8, 512), F32), pltpu.VMEM((Q, N, 32, 128), F32)
    square, pair = pltpu.VMEM((512, 512), BF16), pltpu.VMEM((2, 512, 512), BF16)
    adjoint_next, residual_next = pl.pallas_call(
        kernel,
        out_shape=(field, field),
        in_specs=[hbm] * 9,
        out_specs=(hbm, hbm),
        scratch_shapes=[
            pltpu.VMEM((256, 256), F32),
            pltpu.VMEM((2, 1024, 128), F32),
            pltpu.VMEM((1, 512), F32),
            pltpu.VMEM((1, 512), F32),
            pltpu.VMEM((1, 256), F32),
            pltpu.VMEM((512, 512), F32),
            pltpu.VMEM((512, 512), F32),
            pltpu.VMEM((32, 32, 256), BF16),
            pltpu.VMEM((1024, 256), F32),
            pltpu.VMEM((2, 1024, 256), BF16),
            pltpu.VMEM((2, 1024, 256), BF16),
            pltpu.VMEM((512, 256), BF16),
            pltpu.VMEM((512, 256), BF16),
            square, square, pair, pair, pair, pair,
            pltpu.VMEM((512, 256), BF16),
            pltpu.VMEM((512, 256), BF16),
            pltpu.VMEM((2, 512, 128), F32),
            pltpu.VMEM((Q, 8, 128), F32),
            wide, wide, tall, tall, tall, tall, wide, wide,
            pltpu.VMEM((4, 512, 128), F32),
            pltpu.VMEM((128, 512), F32),
            pltpu.VMEM((2, 2, 1024, 128), F32),
            pltpu.VMEM((2, 38 * ROWS, 128), F32),
            pltpu.VMEM((2, 3, 2, 32, 128), F32),
            pltpu.VMEM((2, 3, 2, ROWS, 128), F32),
            pltpu.VMEM((1024, 512), F32),
            pltpu.SemaphoreType.DMA((10,)),
            pltpu.SemaphoreType.DMA((3,)),
            pltpu.SemaphoreType.DMA((4, Q)),
            pltpu.SemaphoreType.DMA((4, Q)),
            pltpu.SemaphoreType.DMA((12,)),
            pltpu.SemaphoreType.DMA((12,)),
        ],
        compiler_params=pltpu.CompilerParams(
            collective_id=0, has_side_effects=True, vmem_limit_bytes=56 * 1024 * 1024
        ),
    )(
        basis_z, residual.reshape(1024, 256),
        eigen_x.reshape(1, 512), eigen_y.reshape(1, 512), eigen_z.reshape(1, 256),
        basis_x, basis_y, coefficient, adjoint.reshape(1024, 256),
    )
    return adjoint_next.reshape(32, 32, 256), residual_next.reshape(32, 32, 256)


def solution(mesh):
    field = P("row", "col", None)
    return jax.shard_map(
        shards,
        mesh=mesh,
        in_specs=(field, field, field, P(), P(), P(), P(), P(), P()),
        out_specs=(field, field),
        check_vma=False,
    )
```

```python
import jax
import jax.numpy as jnp
from jax import lax
from jax.experimental import pallas as pl
from jax.experimental.pallas import tpu as pltpu
from jax.sharding import PartitionSpec as P

MESH = pl.DeviceIdType.MESH
F32, BF16 = jnp.float32, jnp.bfloat16
N = 16
Q = 4
ROWS = 48
MASS = (2416.0, 1191.0, 120.0, 1.0)
STIFF = (80.0, -15.0, -24.0, -1.0)


def split(x):
    hi = x.astype(BF16)
    return hi, (x - hi.astype(F32)).astype(BF16)


def dot3(a, b, dims=((1,), (0,))):
    (ah, al), (bh, bl) = a, b

    def one(u, v):
        return lax.dot_general(u, v, (dims, ((), ())), preferred_element_type=F32)

    return one(ah, bh) + (one(ah, bl) + one(al, bh))


def transpose4(a):
    lane = lax.broadcasted_iota(jnp.int32, a[0].shape, 1)
    low, even = lane < 64, (lane & 32) == 0
    half = [pltpu.roll(v, 64, 1) for v in a]
    c = [
        jnp.where(low, a[0], half[2]),
        jnp.where(low, a[1], half[3]),
        jnp.where(low, half[0], a[2]),
        jnp.where(low, half[1], a[3]),
    ]
    return [
        jnp.where(even, c[0], pltpu.roll(c[1], 32, 1)),
        jnp.where(even, pltpu.roll(c[0], 96, 1), c[1]),
        jnp.where(even, c[2], pltpu.roll(c[3], 32, 1)),
        jnp.where(even, pltpu.roll(c[2], 96, 1), c[3]),
    ]


def taps(coeffs, scale, planes):
    total = (coeffs[0] * scale) * planes[0]
    for d in range(1, 4):
        total = total + (coeffs[d] * scale) * planes[d]
    return total


def band(coeffs, scale, n):
    i = lax.broadcasted_iota(jnp.int32, (n, n), 0)
    j = lax.broadcasted_iota(jnp.int32, (n, n), 1)
    dist = jnp.abs(i - j)
    total = jnp.zeros((n, n), F32)
    for d in range(4):
        total = jnp.where(dist == d, coeffs[d] * scale, total)
    return total


def kernel(
    bz_hbm, res_hbm, ex_hbm, ey_hbm, ez_hbm, bx_hbm, by_hbm, coef_hbm, adj_hbm,
    adj_out, res_out,
    bz, res, ex, ey, ez, bx, by, coef, adj, dh, dl,
    lh, ll, lmh, lml, bh, bl, bth, btl, zh, zl, ext, rowv,
    send_c, recv_c, send_r, recv_r, send_rb, recv_rb, send_cb, recv_cb,
    fbuf, ubuf, acc, wext, ypack, hext, mixed,
    in_sem, out_sem, send_sem, recv_sem, hsend_sem, hrecv_sem,
):
    r, n = lax.axis_index("row"), lax.axis_index("col")

    loads = [
        pltpu.make_async_copy(src, dst, in_sem.at[s])
        for s, (src, dst) in enumerate(
            (
                (bz_hbm, bz), (res_hbm.at[:, :128], res.at[0]), (res_hbm.at[:, 128:], res.at[1]),
                (bx_hbm, bx), (by_hbm, by), (ex_hbm, ex), (ey_hbm, ey), (ez_hbm, ez), (coef_hbm, coef),
                (adj_hbm, adj),
            )
        )
    ]
    for load in loads:
        load.start()

    barrier = pltpu.get_barrier_semaphore()

    def greet(d, _):
        pl.semaphore_signal(barrier, inc=1, device_id=(r, lax.rem(n + d, N)), device_id_type=MESH)
        pl.semaphore_signal(barrier, inc=1, device_id=(lax.rem(r + d, N), n), device_id_type=MESH)
        return 0

    lax.fori_loop(1, N, greet, 0)
    for dr in (1, N - 1):
        for dn in (1, N - 1):
            pl.semaphore_signal(
                barrier, inc=1, device_id=(lax.rem(r + dr, N), lax.rem(n + dn, N)), device_id_type=MESH
            )

    loads[0].wait()
    top = lax.broadcasted_iota(jnp.int32, (8, 256), 0) < 4

    def prepare(t):
        bzt = bz[:, 128 * t : 128 * t + 128].T
        for p in range(16):
            v = bzt[8 * p : 8 * p + 8, :]
            w = pltpu.roll(v, 4, 0)
            for i, rows in enumerate((jnp.where(top, v, w), jnp.where(top, w, v))):
                at = pl.ds(256 * t + 16 * p + 8 * i, 8)
                fbuf[0, at, :] = rows[:, :128]
                fbuf[1, at, :] = rows[:, 128:]
        at = pl.ds(256 * t, 256)
        lh[at, :], ll[at, :] = split(jnp.concatenate([fbuf[0, at, :], fbuf[1, at, :]], axis=1))

    def exchange(stage, k, src, dst, over_row):
        mine = r if over_row else n

        def one(d, _):
            if over_row:
                peer = lax.rem(r // 8 + d // 8, 2) * 8 + lax.rem(r + d, 8)
            else:
                peer = lax.rem(n // 4 + d // 4, 4) * 4 + lax.rem(n // 2 + d // 2, 2) * 2 + lax.rem(n + d, 2)
            pltpu.make_async_remote_copy(
                src_ref=src.at[k, peer],
                dst_ref=dst.at[k, mine],
                send_sem=send_sem.at[stage, k],
                recv_sem=recv_sem.at[stage, k],
                device_id=(peer, n) if over_row else (r, peer),
                device_id_type=MESH,
            ).start()
            return 0

        lax.fori_loop(1, N, one, 0)
        pltpu.make_async_copy(src.at[k, mine], dst.at[k, mine], recv_sem.at[stage, k]).start()

    def arrived(stage, k, dst):
        pltpu.make_async_copy(dst.at[k], dst.at[k], recv_sem.at[stage, k]).wait()

    loads[1].wait()
    loads[2].wait()
    top16 = lax.broadcasted_iota(jnp.int32, (N, 8, 512), 1) < 4

    def stage_z(t, k):
        rows = (lh[128 * k : 128 * k + 128, :], ll[128 * k : 128 * k + 128, :])
        a, b = (
            dot3(rows, (dh[t, 512 * h : 512 * h + 512, :], dl[t, 512 * h : 512 * h + 512, :]), ((1,), (1,)))
            for h in range(2)
        )
        send_c[k] = jnp.where(top16, a.reshape(N, 8, 512), b.reshape(N, 8, 512))

    dh[1], dl[1] = split(jnp.concatenate([res[0], res[1]], axis=1))
    prepare(1)
    stage_z(1, 2)
    pl.semaphore_wait(barrier, 2 * (N - 1) + 4)
    exchange(0, 2, send_c, recv_c, False)
    for y in range(32):
        plane = jnp.concatenate([res[h, pl.ds(y, 32, stride=32), :] for h in range(2)], axis=1)
        dh[0, 32 * y : 32 * y + 32, :], dl[0, 32 * y : 32 * y + 32, :] = split(plane)
    prepare(0)
    stage_z(0, 0)
    exchange(0, 0, send_c, recv_c, True)
    stage_z(1, 3)
    exchange(0, 3, send_c, recv_c, False)
    stage_z(0, 1)
    exchange(0, 1, send_c, recv_c, True)

    loads[3].wait()
    loads[4].wait()
    for t, basis in enumerate((bx, by)):
        bh[t], bl[t] = split(basis[...])
        bth[t], btl[t] = split(basis[...].T)
    lmat = jnp.concatenate([fbuf[0], fbuf[1]], axis=1)
    half0 = (lax.broadcasted_iota(jnp.int32, (512, 256), 0) & 4) == 0
    lmh[...], lml[...] = split(jnp.concatenate([jnp.where(half0, lmat, 0.0), jnp.where(half0, 0.0, lmat)], axis=1))
    zh[:256, :], zl[:256, :] = split(band(MASS, 1.0 / 5040, 256))
    zh[256:, :], zl[256:, :] = split(band(STIFF, 1.0 / 120, 256))
    for load in loads[5:8]:
        load.wait()
    lane = lax.broadcasted_iota(jnp.int32, (8, 128), 1)
    zlane = lax.broadcasted_iota(jnp.int32, (8, 256), 1)
    ezs = jnp.broadcast_to(ez[...], (8, 256))
    for t, (along, across, block, owner) in enumerate(((ey, ex, n, r), (ex, ey, r, n))):
        ext[t] = jnp.broadcast_to(along[...], (128, 512)).T
        own = pltpu.roll(jnp.broadcast_to(across[...], (8, 512)), lax.rem((N - block) * 32, 512), 1)[:, :128]
        own = jnp.where(lane < 32, own, 0.0)
        own = own + pltpu.roll(own, 32, 1)
        own = own + pltpu.roll(own, 64, 1)
        for k in (2 * t, 2 * t + 1):
            row = own
            for c in range(4):
                one = jnp.sum(jnp.where(zlane == k * 64 + owner * 4 + c, ezs, 0.0), axis=1, keepdims=True)
                row = row + jnp.where((lane >= 32 * c) & (lane < 32 * c + 32), one, 0.0)
            rowv[k] = row

    def first(t, k):
        arrived(0, k, recv_c)
        for g in range(4):
            for y in range(4):
                for u, v in enumerate(
                    transpose4([recv_c[k, 4 * g + m, :, 128 * y : 128 * y + 128] for m in range(4)])
                ):
                    fbuf[g, pl.ds(4 * y + u, 8, stride=16), :] = v
        f = jnp.concatenate([fbuf[g, :128, :] for g in range(4)], axis=1)
        s = dot3(split(f), (bh[t], bl[t]))
        for g in range(4):
            for y in range(2):
                blocks = [s[64 * y + 16 * c : 64 * y + 16 * c + 16, 128 * g : 128 * g + 128] for c in range(4)]
                for m, v in enumerate(transpose4(blocks)):
                    send_r[k, 4 * g + m, 16 * y : 16 * y + 16, :] = v
        exchange(1, k, send_r, recv_r, t == 1)

    def middle(t, k):
        arrived(1, k, recv_r)
        spectrum = dot3((bth[1 - t], btl[1 - t]), split(recv_r[k].reshape(512, 128)))
        scaled = spectrum / (ext[t] + rowv[k][:1, :])
        send_rb[k] = dot3((bh[1 - t], bl[1 - t]), split(scaled)).reshape(N, 32, 128)
        exchange(2, k, send_rb, recv_rb, t == 1)

    def first_back(t, k):
        arrived(2, k, recv_rb)
        for g in range(4):
            for y in range(2):
                blocks = [recv_rb[k, 4 * g + m, 16 * y : 16 * y + 16, :] for m in range(4)]
                for c, v in enumerate(transpose4(blocks)):
                    ubuf[64 * y + 16 * c : 64 * y + 16 * c + 16, 128 * g : 128 * g + 128] = v
        p = dot3(split(ubuf[...]), (bh[t], bl[t]), ((1,), (1,)))
        for g in range(4):
            fbuf[g, :128, :] = p[:, 128 * g : 128 * g + 128]
        for g in range(4):
            for y in range(4):
                blocks = [fbuf[g, pl.ds(4 * y + u, 8, stride=16), :] for u in range(4)]
                for m, v in enumerate(transpose4(blocks)):
                    send_cb[k, 4 * g + m, :, 128 * y : 128 * y + 128] = v
        exchange(3, k, send_cb, recv_cb, t == 0)

    def last(t, k):
        arrived(3, k, recv_cb)
        data = split(recv_cb[k].reshape(128, 512).T)
        rows = pl.ds(pl.multiple_of(128 * k, 128), 128)
        part = dot3(data, (lmh[rows, :], lml[rows, :]))
        for h in range(2):
            for w in range(2):
                at = pl.ds(512 * h, 512)
                acc[t, w, at, :] = acc[t, w, at, :] + part[:, 256 * h + 128 * w : 256 * h + 128 * w + 128]

    acc[...] = jnp.zeros((2, 2, 1024, 128), F32)
    loads[8].wait()
    for x in range(32):
        for h in range(2):
            wext[h, ROWS * (x + 3) + 8 : ROWS * (x + 3) + 40, :] = coef[x, :, 128 * h : 128 * h + 128].astype(F32)
    for side, edge in ((0, 0), (1, 29)):
        for d in range(3):
            for h in range(2):
                ypack[side, d, h] = wext[h, pl.ds(3 * ROWS + 8 + edge + d, 32, stride=ROWS), :]
    for x in range(38):
        for h in range(2):
            wext[h, ROWS * x : ROWS * x + 8, :] = jnp.zeros((8, 128), F32)
            wext[h, ROWS * x + 40 : ROWS * x + 48, :] = jnp.zeros((8, 128), F32)

    def pairs(*steps):
        def one(j, _):
            for stage, t in steps:
                stage(t, 2 * t + j)
            return 0

        lax.fori_loop(0, 2, one, 0)

    pairs((first, 1), (first, 0))
    pairs((middle, 0), (middle, 1))
    pairs((first_back, 0))
    pairs((first_back, 1))
    pairs((last, 1), (last, 0))

    def weigh(x):
        for h in range(2):
            c = acc[0, h, pl.ds(x, 32, stride=32), :] + acc[1, h, 32 * x : 32 * x + 32, :]
            at = slice(ROWS * (x + 3) + 8, ROWS * (x + 3) + 40)
            wext[h, at, :] = wext[h, at, :] * c

    for side, edge in ((0, 0), (1, 29)):
        for d in range(3):
            for h in range(2):
                y = edge + d
                c = acc[0, h, 32 * y : 32 * y + 32, :] + acc[1, h, pl.ds(y, 32, stride=32), :]
                ypack[side, d, h] = ypack[side, d, h] * c

    has = {(0, 0): None}
    for dr in (-1, 0, 1):
        for dn in (-1, 0, 1):
            ok_r = (r > 0) if dr < 0 else (r < N - 1)
            ok_n = (n > 0) if dn < 0 else (n < N - 1)
            has[dr, dn] = ok_n if dr == 0 else ok_r if dn == 0 else ok_r & ok_n

    def copies(dr, dn):
        peer = (r + dr, n + dn)
        out = []
        if dn == 0:
            for d in range(3):
                src = pl.ds(ROWS * ((3 if dr < 0 else 32) + d) + 8, 32)
                dst = pl.ds(ROWS * ((35 if dr < 0 else 0) + d) + 8, 32)
                out.append((wext.at[:, src, :], wext.at[:, dst, :], (0 if dr < 0 else 3) + d))
        elif dr == 0:
            side = 0 if dn < 0 else 1
            for d in range(3):
                out.append((ypack.at[side, d], hext.at[1 - side, d, :, pl.ds(8, 32), :], 6 + 3 * side + d))
        else:
            side = 0 if dn < 0 else 1
            rows, at = (0, 40) if dr < 0 else (24, 0)
            out.append(
                (
                    ypack.at[side, :, :, pl.ds(rows, 8), :],
                    hext.at[1 - side, :, :, pl.ds(at, 8), :],
                    12 + 2 * (dr > 0) + side,
                )
            )
        return [
            pltpu.make_async_remote_copy(
                src_ref=a, dst_ref=b, send_sem=hsend_sem.at[s], recv_sem=hrecv_sem.at[s],
                device_id=peer, device_id_type=MESH,
            )
            for a, b, s in out
        ]

    sides = [(dr, dn) for dr in (-1, 0, 1) for dn in (-1, 0, 1) if (dr, dn) != (0, 0)]
    def send(some):
        for dr, dn in some:

            @pl.when(has[dr, dn])
            def _():
                for c in copies(dr, dn):
                    c.start()

    send([d for d in sides if d[0] == 0])
    for x in (0, 1, 2, 29, 30, 31):
        weigh(x)
    send([d for d in sides if d[0] != 0])
    for x in range(3, 29):
        weigh(x)

    for dr in (-1, 1):

        @pl.when(jnp.logical_not(has[dr, 0]))
        def _():
            for d in range(3):
                at = pl.ds(ROWS * ((0 if dr < 0 else 35) + d) + 8, 32)
                for h in range(2):
                    wext[h, at, :] = jnp.zeros((32, 128), F32)

    for dn in (-1, 1):

        @pl.when(jnp.logical_not(has[0, dn]))
        def _():
            hext[0 if dn < 0 else 1, :, :, 8:40, :] = jnp.zeros((3, 2, 32, 128), F32)

        for dr in (-1, 1):

            @pl.when(jnp.logical_not(has[dr, dn]))
            def _():
                at = 0 if dr < 0 else 40
                hext[0 if dn < 0 else 1, :, :, at : at + 8, :] = jnp.zeros((3, 2, 8, 128), F32)

    def receive(some):
        for dr, dn in some:

            @pl.when(has[dr, dn])
            def _():
                for c in copies(-dr, -dn):
                    c.wait_recv()

    def along_rows(v):
        return [v[8:40]] + [pltpu.roll(v, d, 0)[8:40] + pltpu.roll(v, ROWS - d, 0)[8:40] for d in range(1, 4)]

    def stencil(x, _):
        base = pl.multiple_of(x * ROWS, 8)
        for h in range(2):
            p = [wext[h, pl.ds(base + ROWS * i, ROWS), :] for i in range(7)]
            sums = [p[3], p[2] + p[4], p[1] + p[5], p[0] + p[6]]

            mass = along_rows(taps(MASS, 1.0 / 5040, sums))
            stiff = along_rows(taps(STIFF, 1.0 / 120, sums))
            at = pl.ds(pl.multiple_of(x * 32, 32), 32)
            mixed[at, 128 * h : 128 * h + 128] = taps(STIFF, 1.0 / 120, mass) + taps(MASS, 1.0 / 5040, stiff)
            mixed[at, 256 + 128 * h : 256 + 128 * h + 128] = taps(MASS, 1.0 / 5040, mass)
        return 0

    def finish(i):
        at = slice(256 * i, 256 * i + 256)
        image = dot3(split(mixed[at, :]), (zh[...], zl[...]))
        for h in range(2):
            res[h, at, :] = res[h, at, :] - image[:, 128 * h : 128 * h + 128]

    lax.fori_loop(3, 29, stencil, 0)
    finish(1)
    finish(2)
    loads[9].wait()
    for x in range(32):
        for h in range(2):
            c = acc[0, h, pl.ds(x, 32, stride=32), :] + acc[1, h, 32 * x : 32 * x + 32, :]
            at = slice(128 * h, 128 * h + 128)
            adj[32 * x : 32 * x + 32, at] = adj[32 * x : 32 * x + 32, at] + c
    stores = [pltpu.make_async_copy(adj, adj_out, out_sem.at[0])]
    stores[0].start()
    receive([d for d in sides if d[1] == 0])
    lax.fori_loop(0, 3, stencil, 0)
    finish(0)
    lax.fori_loop(29, 32, stencil, 0)
    finish(3)

    receive([d for d in sides if d[1] != 0])
    for side in range(2):
        for h in range(2):
            near = [along_rows(hext[side, d, h]) for d in range(3)]
            mass = [taps(MASS, 1.0 / 5040, v) for v in near]
            stiff = [taps(STIFF, 1.0 / 120, v) for v in near]
            for o in range(3):
                a = b = jnp.zeros((32, 128), F32)
                for d in range(o, 3) if side == 0 else range(o + 1):
                    dist = o + 3 - d if side == 0 else 3 + d - o
                    a = a + (STIFF[dist] / 120) * mass[d] + (MASS[dist] / 5040) * stiff[d]
                    b = b + (MASS[dist] / 5040) * mass[d]
                at = slice(96 * side + 32 * o, 96 * side + 32 * o + 32)
                mixed[at, 128 * h : 128 * h + 128] = a
                mixed[at, 256 + 128 * h : 256 + 128 * h + 128] = b
    image = dot3(split(mixed[:192, :]), (zh[...], zl[...]))
    for h in range(2):
        for side in range(2):
            for o in range(3):
                at = pl.ds(o if side == 0 else 29 + o, 32, stride=32)
                part = image[96 * side + 32 * o : 96 * side + 32 * o + 32, 128 * h : 128 * h + 128]
                res[h, at, :] = res[h, at, :] - part
        store = pltpu.make_async_copy(res.at[h], res_out.at[:, pl.ds(128 * h, 128)], out_sem.at[1 + h])
        store.start()
        stores.append(store)

    for dr, dn in sides:

        @pl.when(has[dr, dn])
        def _():
            for c in copies(dr, dn):
                c.wait_send()

    for stage, src in enumerate((send_c, send_r, send_rb, send_cb)):
        for k in range(Q):
            sent = src.at[k, pl.ds(0, N - 1)]
            pltpu.make_async_copy(sent, sent, send_sem.at[stage, k]).wait()

    for store in stores:
        store.wait()


def shards(residual, adjoint, coefficient, basis_x, basis_y, basis_z, eigen_x, eigen_y, eigen_z):
    field = jax.ShapeDtypeStruct((1024, 256), F32)
    hbm = pl.BlockSpec(memory_space=pltpu.HBM)
    wide, tall = pltpu.VMEM((Q, N, 8, 512), F32), pltpu.VMEM((Q, N, 32, 128), F32)
    square, pair = pltpu.VMEM((512, 512), BF16), pltpu.VMEM((2, 512, 512), BF16)
    adjoint_next, residual_next = pl.pallas_call(
        kernel,
        out_shape=(field, field),
        in_specs=[hbm] * 9,
        out_specs=(hbm, hbm),
        scratch_shapes=[
            pltpu.VMEM((256, 256), F32),
            pltpu.VMEM((2, 1024, 128), F32),
            pltpu.VMEM((1, 512), F32),
            pltpu.VMEM((1, 512), F32),
            pltpu.VMEM((1, 256), F32),
            pltpu.VMEM((512, 512), F32),
            pltpu.VMEM((512, 512), F32),
            pltpu.VMEM((32, 32, 256), BF16),
            pltpu.VMEM((1024, 256), F32),
            pltpu.VMEM((2, 1024, 256), BF16),
            pltpu.VMEM((2, 1024, 256), BF16),
            pltpu.VMEM((512, 256), BF16),
            pltpu.VMEM((512, 256), BF16),
            square, square, pair, pair, pair, pair,
            pltpu.VMEM((512, 256), BF16),
            pltpu.VMEM((512, 256), BF16),
            pltpu.VMEM((2, 512, 128), F32),
            pltpu.VMEM((Q, 8, 128), F32),
            wide, wide, tall, tall, tall, tall, wide, wide,
            pltpu.VMEM((4, 512, 128), F32),
            pltpu.VMEM((128, 512), F32),
            pltpu.VMEM((2, 2, 1024, 128), F32),
            pltpu.VMEM((2, 38 * ROWS, 128), F32),
            pltpu.VMEM((2, 3, 2, 32, 128), F32),
            pltpu.VMEM((2, 3, 2, ROWS, 128), F32),
            pltpu.VMEM((1024, 512), F32),
            pltpu.SemaphoreType.DMA((10,)),
            pltpu.SemaphoreType.DMA((3,)),
            pltpu.SemaphoreType.DMA((4, Q)),
            pltpu.SemaphoreType.DMA((4, Q)),
            pltpu.SemaphoreType.DMA((16,)),
            pltpu.SemaphoreType.DMA((16,)),
        ],
        compiler_params=pltpu.CompilerParams(
            collective_id=0, has_side_effects=True, vmem_limit_bytes=56 * 1024 * 1024
        ),
    )(
        basis_z, residual.reshape(1024, 256),
        eigen_x.reshape(1, 512), eigen_y.reshape(1, 512), eigen_z.reshape(1, 256),
        basis_x, basis_y, coefficient, adjoint.reshape(1024, 256),
    )
    return adjoint_next.reshape(32, 32, 256), residual_next.reshape(32, 32, 256)


def solution(mesh):
    field = P("row", "col", None)
    return jax.shard_map(
        shards,
        mesh=mesh,
        in_specs=(field, field, field, P(), P(), P(), P(), P(), P()),
        out_specs=(field, field),
        check_vma=False,
    )
```

```python
import jax
import jax.numpy as jnp
from jax import lax
from jax.experimental import pallas as pl
from jax.experimental.pallas import tpu as pltpu
from jax.sharding import PartitionSpec as P

MESH = pl.DeviceIdType.MESH
F32, BF16 = jnp.float32, jnp.bfloat16
N = 16
Q = 4
ROWS = 48
MASS = (2416.0, 1191.0, 120.0, 1.0)
STIFF = (80.0, -15.0, -24.0, -1.0)


def split(x):
    hi = x.astype(BF16)
    return hi, (x - hi.astype(F32)).astype(BF16)


def dot3(a, b, dims=((1,), (0,))):
    (ah, al), (bh, bl) = a, b

    def one(u, v):
        return lax.dot_general(u, v, (dims, ((), ())), preferred_element_type=F32)

    return one(ah, bh) + (one(ah, bl) + one(al, bh))


def transpose4(a):
    lane = lax.broadcasted_iota(jnp.int32, a[0].shape, 1)
    low, even = lane < 64, (lane & 32) == 0
    half = [pltpu.roll(v, 64, 1) for v in a]
    c = [
        jnp.where(low, a[0], half[2]),
        jnp.where(low, a[1], half[3]),
        jnp.where(low, half[0], a[2]),
        jnp.where(low, half[1], a[3]),
    ]
    return [
        jnp.where(even, c[0], pltpu.roll(c[1], 32, 1)),
        jnp.where(even, pltpu.roll(c[0], 96, 1), c[1]),
        jnp.where(even, c[2], pltpu.roll(c[3], 32, 1)),
        jnp.where(even, pltpu.roll(c[2], 96, 1), c[3]),
    ]


def taps(coeffs, scale, planes):
    total = (coeffs[0] * scale) * planes[0]
    for d in range(1, 4):
        total = total + (coeffs[d] * scale) * planes[d]
    return total


def band(coeffs, scale, n):
    i = lax.broadcasted_iota(jnp.int32, (n, n), 0)
    j = lax.broadcasted_iota(jnp.int32, (n, n), 1)
    dist = jnp.abs(i - j)
    total = jnp.zeros((n, n), F32)
    for d in range(4):
        total = jnp.where(dist == d, coeffs[d] * scale, total)
    return total


def kernel(
    bz_hbm, res_hbm, ex_hbm, ey_hbm, ez_hbm, bx_hbm, by_hbm, coef_hbm, adj_hbm,
    adj_out, res_out,
    bz, res, ex, ey, ez, bx, by, coef, adj, dh, dl,
    lh, ll, lmh, lml, bh, bl, bth, btl, zh, zl, ext, rowv,
    send_c, recv_c, send_r, recv_r, send_rb, recv_rb, send_cb, recv_cb,
    fbuf, ubuf, acc, wext, ypack, hext, mixed,
    in_sem, out_sem, send_sem, recv_sem, hsend_sem, hrecv_sem,
):
    r, n = lax.axis_index("row"), lax.axis_index("col")

    loads = [
        pltpu.make_async_copy(src, dst, in_sem.at[s])
        for s, (src, dst) in enumerate(
            (
                (bz_hbm, bz), (res_hbm.at[:, :128], res.at[0, :1024]), (res_hbm.at[:, 128:], res.at[1, :1024]),
                (bx_hbm, bx), (by_hbm, by), (ex_hbm, ex), (ey_hbm, ey), (ez_hbm, ez), (coef_hbm, coef),
                (adj_hbm, adj),
            )
        )
    ]
    for load in loads:
        load.start()

    barrier = pltpu.get_barrier_semaphore()

    def greet(d, _):
        pl.semaphore_signal(barrier, inc=1, device_id=(r, lax.rem(n + d, N)), device_id_type=MESH)
        pl.semaphore_signal(barrier, inc=1, device_id=(lax.rem(r + d, N), n), device_id_type=MESH)
        return 0

    lax.fori_loop(1, N, greet, 0)
    for dr in (1, N - 1):
        for dn in (1, N - 1):
            pl.semaphore_signal(
                barrier, inc=1, device_id=(lax.rem(r + dr, N), lax.rem(n + dn, N)), device_id_type=MESH
            )

    loads[0].wait()
    top = lax.broadcasted_iota(jnp.int32, (8, 256), 0) < 4

    def prepare(t):
        bzt = bz[:, 128 * t : 128 * t + 128].T
        for p in range(16):
            v = bzt[8 * p : 8 * p + 8, :]
            w = pltpu.roll(v, 4, 0)
            for i, rows in enumerate((jnp.where(top, v, w), jnp.where(top, w, v))):
                at = pl.ds(256 * t + 16 * p + 8 * i, 8)
                fbuf[0, at, :] = rows[:, :128]
                fbuf[1, at, :] = rows[:, 128:]
        at = pl.ds(256 * t, 256)
        lh[at, :], ll[at, :] = split(jnp.concatenate([fbuf[0, at, :], fbuf[1, at, :]], axis=1))

    def exchange(stage, k, src, dst, over_row):
        mine = r if over_row else n

        def one(d, _):
            if over_row:
                peer = lax.rem(r // 8 + d // 8, 2) * 8 + lax.rem(r + d, 8)
            else:
                peer = lax.rem(n // 4 + d // 4, 4) * 4 + lax.rem(n // 2 + d // 2, 2) * 2 + lax.rem(n + d, 2)
            pltpu.make_async_remote_copy(
                src_ref=src.at[k, peer],
                dst_ref=dst.at[k, mine],
                send_sem=send_sem.at[stage, k],
                recv_sem=recv_sem.at[stage, k],
                device_id=(peer, n) if over_row else (r, peer),
                device_id_type=MESH,
            ).start()
            return 0

        lax.fori_loop(1, N, one, 0)
        pltpu.make_async_copy(src.at[k, mine], dst.at[k, mine], recv_sem.at[stage, k]).start()

    def arrived(stage, k, dst):
        pltpu.make_async_copy(dst.at[k], dst.at[k], recv_sem.at[stage, k]).wait()

    loads[1].wait()
    loads[2].wait()
    top16 = lax.broadcasted_iota(jnp.int32, (N, 8, 512), 1) < 4

    def stage_z(t, k):
        rows = (lh[128 * k : 128 * k + 128, :], ll[128 * k : 128 * k + 128, :])
        a, b = (
            dot3(rows, (dh[t, 512 * h : 512 * h + 512, :], dl[t, 512 * h : 512 * h + 512, :]), ((1,), (1,)))
            for h in range(2)
        )
        send_c[k] = jnp.where(top16, a.reshape(N, 8, 512), b.reshape(N, 8, 512))

    dh[1], dl[1] = split(jnp.concatenate([res[0, :1024], res[1, :1024]], axis=1))
    prepare(1)
    stage_z(1, 2)
    pl.semaphore_wait(barrier, 2 * (N - 1) + 4)
    exchange(0, 2, send_c, recv_c, False)
    for y in range(32):
        plane = jnp.concatenate([res[h, pl.ds(y, 32, stride=32), :] for h in range(2)], axis=1)
        dh[0, 32 * y : 32 * y + 32, :], dl[0, 32 * y : 32 * y + 32, :] = split(plane)
    prepare(0)
    stage_z(0, 0)
    exchange(0, 0, send_c, recv_c, True)
    stage_z(1, 3)
    exchange(0, 3, send_c, recv_c, False)
    stage_z(0, 1)
    exchange(0, 1, send_c, recv_c, True)

    loads[3].wait()
    loads[4].wait()
    for t, basis in enumerate((bx, by)):
        bh[t], bl[t] = split(basis[...])
        bth[t], btl[t] = split(basis[...].T)
    lmat = jnp.concatenate([fbuf[0], fbuf[1]], axis=1)
    half0 = (lax.broadcasted_iota(jnp.int32, (512, 256), 0) & 4) == 0
    lmh[...], lml[...] = split(jnp.concatenate([jnp.where(half0, lmat, 0.0), jnp.where(half0, 0.0, lmat)], axis=1))
    zh[:256, :], zl[:256, :] = split(band(MASS, 1.0 / 5040, 256))
    zh[256:, :], zl[256:, :] = split(band(STIFF, 1.0 / 120, 256))
    for load in loads[5:8]:
        load.wait()
    lane = lax.broadcasted_iota(jnp.int32, (8, 128), 1)
    zlane = lax.broadcasted_iota(jnp.int32, (8, 256), 1)
    ezs = jnp.broadcast_to(ez[...], (8, 256))
    for t, (along, across, block, owner) in enumerate(((ey, ex, n, r), (ex, ey, r, n))):
        ext[t] = jnp.broadcast_to(along[...], (128, 512)).T
        own = pltpu.roll(jnp.broadcast_to(across[...], (8, 512)), lax.rem((N - block) * 32, 512), 1)[:, :128]
        own = jnp.where(lane < 32, own, 0.0)
        own = own + pltpu.roll(own, 32, 1)
        own = own + pltpu.roll(own, 64, 1)
        for k in (2 * t, 2 * t + 1):
            row = own
            for c in range(4):
                one = jnp.sum(jnp.where(zlane == k * 64 + owner * 4 + c, ezs, 0.0), axis=1, keepdims=True)
                row = row + jnp.where((lane >= 32 * c) & (lane < 32 * c + 32), one, 0.0)
            rowv[k] = row

    def first(t, k):
        arrived(0, k, recv_c)
        for g in range(4):
            for y in range(4):
                for u, v in enumerate(
                    transpose4([recv_c[k, 4 * g + m, :, 128 * y : 128 * y + 128] for m in range(4)])
                ):
                    fbuf[g, pl.ds(4 * y + u, 8, stride=16), :] = v
        f = jnp.concatenate([fbuf[g, :128, :] for g in range(4)], axis=1)
        s = dot3(split(f), (bh[t], bl[t]))
        for g in range(4):
            for y in range(2):
                blocks = [s[64 * y + 16 * c : 64 * y + 16 * c + 16, 128 * g : 128 * g + 128] for c in range(4)]
                for m, v in enumerate(transpose4(blocks)):
                    send_r[k, 4 * g + m, 16 * y : 16 * y + 16, :] = v
        exchange(1, k, send_r, recv_r, t == 1)

    def middle(t, k):
        arrived(1, k, recv_r)
        spectrum = dot3((bth[1 - t], btl[1 - t]), split(recv_r[k].reshape(512, 128)))
        scaled = spectrum / (ext[t] + rowv[k][:1, :])
        send_rb[k] = dot3((bh[1 - t], bl[1 - t]), split(scaled)).reshape(N, 32, 128)
        exchange(2, k, send_rb, recv_rb, t == 1)

    def first_back(t, k):
        arrived(2, k, recv_rb)
        for g in range(4):
            for y in range(2):
                blocks = [recv_rb[k, 4 * g + m, 16 * y : 16 * y + 16, :] for m in range(4)]
                for c, v in enumerate(transpose4(blocks)):
                    ubuf[64 * y + 16 * c : 64 * y + 16 * c + 16, 128 * g : 128 * g + 128] = v
        p = dot3(split(ubuf[...]), (bh[t], bl[t]), ((1,), (1,)))
        for g in range(4):
            fbuf[g, :128, :] = p[:, 128 * g : 128 * g + 128]
        for g in range(4):
            for y in range(4):
                blocks = [fbuf[g, pl.ds(4 * y + u, 8, stride=16), :] for u in range(4)]
                for m, v in enumerate(transpose4(blocks)):
                    send_cb[k, 4 * g + m, :, 128 * y : 128 * y + 128] = v
        exchange(3, k, send_cb, recv_cb, t == 0)

    def last(t, k):
        arrived(3, k, recv_cb)
        data = split(recv_cb[k].reshape(128, 512).T)
        rows = pl.ds(pl.multiple_of(128 * k, 128), 128)
        part = dot3(data, (lmh[rows, :], lml[rows, :]))
        for h in range(2):
            for w in range(2):
                at = pl.ds(512 * h, 512)
                acc[t, w, at, :] = acc[t, w, at, :] + part[:, 256 * h + 128 * w : 256 * h + 128 * w + 128]

    acc[...] = jnp.zeros((2, 2, 1056, 128), F32)
    loads[8].wait()
    for x in range(32):
        for h in range(2):
            wext[h, ROWS * (x + 3) + 8 : ROWS * (x + 3) + 40, :] = coef[x, :, 128 * h : 128 * h + 128].astype(F32)
    for side, edge in ((0, 0), (1, 29)):
        for d in range(3):
            for h in range(2):
                ypack[side, d, h] = wext[h, pl.ds(3 * ROWS + 8 + edge + d, 32, stride=ROWS), :]
    for x in range(38):
        for h in range(2):
            wext[h, ROWS * x : ROWS * x + 8, :] = jnp.zeros((8, 128), F32)
            wext[h, ROWS * x + 40 : ROWS * x + 48, :] = jnp.zeros((8, 128), F32)

    def pairs(*steps):
        def one(j, _):
            for stage, t in steps:
                stage(t, 2 * t + j)
            return 0

        lax.fori_loop(0, 2, one, 0)

    pairs((first, 1), (first, 0))
    pairs((middle, 0), (middle, 1))
    pairs((first_back, 0), (first_back, 1))
    pairs((last, 1), (last, 0))

    def weigh(x):
        for h in range(2):
            c = acc[0, h, pl.ds(x, 32, stride=32), :] + acc[1, h, 32 * x : 32 * x + 32, :]
            at = slice(ROWS * (x + 3) + 8, ROWS * (x + 3) + 40)
            wext[h, at, :] = wext[h, at, :] * c

    for side, edge in ((0, 0), (1, 29)):
        for d in range(3):
            for h in range(2):
                y = edge + d
                c = acc[0, h, 32 * y : 32 * y + 32, :] + acc[1, h, pl.ds(y, 32, stride=32), :]
                ypack[side, d, h] = ypack[side, d, h] * c

    has = {(0, 0): None}
    for dr in (-1, 0, 1):
        for dn in (-1, 0, 1):
            ok_r = (r > 0) if dr < 0 else (r < N - 1)
            ok_n = (n > 0) if dn < 0 else (n < N - 1)
            has[dr, dn] = ok_n if dr == 0 else ok_r if dn == 0 else ok_r & ok_n

    def copies(dr, dn):
        peer = (r + dr, n + dn)
        out = []
        if dn == 0:
            for d in range(3):
                src = pl.ds(ROWS * ((3 if dr < 0 else 32) + d) + 8, 32)
                dst = pl.ds(ROWS * ((35 if dr < 0 else 0) + d) + 8, 32)
                out.append((wext.at[:, src, :], wext.at[:, dst, :], (0 if dr < 0 else 3) + d))
        elif dr == 0:
            side = 0 if dn < 0 else 1
            for d in range(3):
                out.append((ypack.at[side, d], hext.at[1 - side, d, :, pl.ds(8, 32), :], 6 + 3 * side + d))
        else:
            side = 0 if dn < 0 else 1
            rows, at = (0, 40) if dr < 0 else (24, 0)
            out.append(
                (
                    ypack.at[side, :, :, pl.ds(rows, 8), :],
                    hext.at[1 - side, :, :, pl.ds(at, 8), :],
                    12 + 2 * (dr > 0) + side,
                )
            )
        return [
            pltpu.make_async_remote_copy(
                src_ref=a, dst_ref=b, send_sem=hsend_sem.at[s], recv_sem=hrecv_sem.at[s],
                device_id=peer, device_id_type=MESH,
            )
            for a, b, s in out
        ]

    sides = [(dr, dn) for dr in (-1, 0, 1) for dn in (-1, 0, 1) if (dr, dn) != (0, 0)]
    def send(some):
        for dr, dn in some:

            @pl.when(has[dr, dn])
            def _():
                for c in copies(dr, dn):
                    c.start()

    send([d for d in sides if d[0] == 0])
    for x in (0, 1, 2, 29, 30, 31):
        weigh(x)
    send([d for d in sides if d[0] != 0])
    for x in range(3, 29):
        weigh(x)

    for dr in (-1, 1):

        @pl.when(jnp.logical_not(has[dr, 0]))
        def _():
            for d in range(3):
                at = pl.ds(ROWS * ((0 if dr < 0 else 35) + d) + 8, 32)
                for h in range(2):
                    wext[h, at, :] = jnp.zeros((32, 128), F32)

    for dn in (-1, 1):

        @pl.when(jnp.logical_not(has[0, dn]))
        def _():
            hext[0 if dn < 0 else 1, :, :, 8:40, :] = jnp.zeros((3, 2, 32, 128), F32)

        for dr in (-1, 1):

            @pl.when(jnp.logical_not(has[dr, dn]))
            def _():
                at = 0 if dr < 0 else 40
                hext[0 if dn < 0 else 1, :, :, at : at + 8, :] = jnp.zeros((3, 2, 8, 128), F32)

    def receive(some):
        for dr, dn in some:

            @pl.when(has[dr, dn])
            def _():
                for c in copies(-dr, -dn):
                    c.wait_recv()

    def along_rows(v):
        return [v[8:40]] + [pltpu.roll(v, d, 0)[8:40] + pltpu.roll(v, ROWS - d, 0)[8:40] for d in range(1, 4)]

    def stencil(x, _):
        base = pl.multiple_of(x * ROWS, 8)
        for h in range(2):
            p = [wext[h, pl.ds(base + ROWS * i, ROWS), :] for i in range(7)]
            sums = [p[3], p[2] + p[4], p[1] + p[5], p[0] + p[6]]

            mass = along_rows(taps(MASS, 1.0 / 5040, sums))
            stiff = along_rows(taps(STIFF, 1.0 / 120, sums))
            at = pl.ds(pl.multiple_of(x * 32, 32), 32)
            mixed[at, 128 * h : 128 * h + 128] = taps(STIFF, 1.0 / 120, mass) + taps(MASS, 1.0 / 5040, stiff)
            mixed[at, 256 + 128 * h : 256 + 128 * h + 128] = taps(MASS, 1.0 / 5040, mass)
        return 0

    def finish(i):
        at = slice(256 * i, 256 * i + 256)
        image = dot3(split(mixed[at, :]), (zh[...], zl[...]))
        for h in range(2):
            res[h, at, :] = res[h, at, :] - image[:, 128 * h : 128 * h + 128]

    lax.fori_loop(3, 29, stencil, 0)
    finish(1)
    finish(2)
    loads[9].wait()
    for x in range(32):
        for h in range(2):
            c = acc[0, h, pl.ds(x, 32, stride=32), :] + acc[1, h, 32 * x : 32 * x + 32, :]
            at = slice(128 * h, 128 * h + 128)
            adj[32 * x : 32 * x + 32, at] = adj[32 * x : 32 * x + 32, at] + c
    stores = [pltpu.make_async_copy(adj, adj_out, out_sem.at[0])]
    stores[0].start()
    receive([d for d in sides if d[1] == 0])
    lax.fori_loop(0, 3, stencil, 0)
    finish(0)
    lax.fori_loop(29, 32, stencil, 0)
    finish(3)

    receive([d for d in sides if d[1] != 0])
    for side in range(2):
        for h in range(2):
            near = [along_rows(hext[side, d, h]) for d in range(3)]
            mass = [taps(MASS, 1.0 / 5040, v) for v in near]
            stiff = [taps(STIFF, 1.0 / 120, v) for v in near]
            for o in range(3):
                a = b = jnp.zeros((32, 128), F32)
                for d in range(o, 3) if side == 0 else range(o + 1):
                    dist = o + 3 - d if side == 0 else 3 + d - o
                    a = a + (STIFF[dist] / 120) * mass[d] + (MASS[dist] / 5040) * stiff[d]
                    b = b + (MASS[dist] / 5040) * mass[d]
                at = slice(96 * side + 32 * o, 96 * side + 32 * o + 32)
                mixed[at, 128 * h : 128 * h + 128] = a
                mixed[at, 256 + 128 * h : 256 + 128 * h + 128] = b
    image = dot3(split(mixed[:192, :]), (zh[...], zl[...]))
    for h in range(2):
        for side in range(2):
            for o in range(3):
                at = pl.ds(o if side == 0 else 29 + o, 32, stride=32)
                part = image[96 * side + 32 * o : 96 * side + 32 * o + 32, 128 * h : 128 * h + 128]
                res[h, at, :] = res[h, at, :] - part
        store = pltpu.make_async_copy(res.at[h, :1024], res_out.at[:, pl.ds(128 * h, 128)], out_sem.at[1 + h])
        store.start()
        stores.append(store)

    for dr, dn in sides:

        @pl.when(has[dr, dn])
        def _():
            for c in copies(dr, dn):
                c.wait_send()

    for stage, src in enumerate((send_c, send_r, send_rb, send_cb)):
        for k in range(Q):
            sent = src.at[k, pl.ds(0, N - 1)]
            pltpu.make_async_copy(sent, sent, send_sem.at[stage, k]).wait()

    for store in stores:
        store.wait()


def shards(residual, adjoint, coefficient, basis_x, basis_y, basis_z, eigen_x, eigen_y, eigen_z):
    field = jax.ShapeDtypeStruct((1024, 256), F32)
    hbm = pl.BlockSpec(memory_space=pltpu.HBM)
    wide, tall = pltpu.VMEM((Q, N, 8, 512), F32), pltpu.VMEM((Q, N, 32, 128), F32)
    square, pair = pltpu.VMEM((512, 512), BF16), pltpu.VMEM((2, 512, 512), BF16)
    adjoint_next, residual_next = pl.pallas_call(
        kernel,
        out_shape=(field, field),
        in_specs=[hbm] * 9,
        out_specs=(hbm, hbm),
        scratch_shapes=[
            pltpu.VMEM((256, 256), F32),
            pltpu.VMEM((2, 1056, 128), F32),
            pltpu.VMEM((1, 512), F32),
            pltpu.VMEM((1, 512), F32),
            pltpu.VMEM((1, 256), F32),
            pltpu.VMEM((512, 512), F32),
            pltpu.VMEM((512, 512), F32),
            pltpu.VMEM((32, 32, 256), BF16),
            pltpu.VMEM((1024, 256), F32),
            pltpu.VMEM((2, 1024, 256), BF16),
            pltpu.VMEM((2, 1024, 256), BF16),
            pltpu.VMEM((512, 256), BF16),
            pltpu.VMEM((512, 256), BF16),
            square, square, pair, pair, pair, pair,
            pltpu.VMEM((512, 256), BF16),
            pltpu.VMEM((512, 256), BF16),
            pltpu.VMEM((2, 512, 128), F32),
            pltpu.VMEM((Q, 8, 128), F32),
            wide, wide, tall, tall, tall, tall, wide, wide,
            pltpu.VMEM((4, 512, 128), F32),
            pltpu.VMEM((128, 512), F32),
            pltpu.VMEM((2, 2, 1056, 128), F32),
            pltpu.VMEM((2, 38 * ROWS, 128), F32),
            pltpu.VMEM((2, 3, 2, 32, 128), F32),
            pltpu.VMEM((2, 3, 2, ROWS, 128), F32),
            pltpu.VMEM((1024, 512), F32),
            pltpu.SemaphoreType.DMA((10,)),
            pltpu.SemaphoreType.DMA((3,)),
            pltpu.SemaphoreType.DMA((4, Q)),
            pltpu.SemaphoreType.DMA((4, Q)),
            pltpu.SemaphoreType.DMA((16,)),
            pltpu.SemaphoreType.DMA((16,)),
        ],
        compiler_params=pltpu.CompilerParams(
            collective_id=0, has_side_effects=True, vmem_limit_bytes=56 * 1024 * 1024
        ),
    )(
        basis_z, residual.reshape(1024, 256),
        eigen_x.reshape(1, 512), eigen_y.reshape(1, 512), eigen_z.reshape(1, 256),
        basis_x, basis_y, coefficient, adjoint.reshape(1024, 256),
    )
    return adjoint_next.reshape(32, 32, 256), residual_next.reshape(32, 32, 256)


def solution(mesh):
    field = P("row", "col", None)
    return jax.shard_map(
        shards,
        mesh=mesh,
        in_specs=(field, field, field, P(), P(), P(), P(), P(), P()),
        out_specs=(field, field),
        check_vma=False,
    )
```
